512 devices in a mesh: patch: 16 (over y_lo, x), dir: 32 (over y_hi, z, core).
Axes of the slice: x: 4, y: 8 (y_hi: 2, y_lo: 4; y = y_hi * 4 + y_lo), z: 8, core: 2. Of those that a mesh axis runs over, the one named last changes fastest.
Arguments:
- fine_out: bfloat16 [96, 128, 2, 4, 512], P('patch', 'dir'), may hold values from -6 to 6
- interp: bfloat16 [512, 2048], replicated, may hold values from -0.25 to 0.25
- child_phase: float32 [4, 2048], replicated, may hold values from -3.140625 to 3.140625
- fine_ops: float32 [40, 2, 512], replicated, may hold values from -1.2 to 1.2
- parent_ops: float32 [40, 2, 2048], P(None, None, 'dir'), may hold values from -0.6 to 0.6
- fine_src: int32 [96, 128, 32], P('patch'), may hold values from 0 to 12287, as said below
- fine_op: int32 [96, 128, 32], P('patch'), may hold values from 0 to 40, as said below
- parent_src: int32 [48, 64, 32], P('patch'), may hold values from 0 to 3071, as said below
- parent_op: int32 [48, 64, 32], P('patch'), may hold values from 0 to 40, as said below
Outputs:
- fine_in: float32 [96, 128, 2, 4, 512], P('patch', 'dir')
The draws below stay inside these ranges and needn't reach their ends.
Inputs may be any that keep to these rules, and one draw needn't show every extreme that they name: `fine_src`: A slot with op id 40 is padding and names the box itself. Every other slot names a distinct box at most 3 rows and 3 columns away, not adjacent to the box, whose parent is adjacent to or equal to the box's parent; its op id is the index of the offset (dr, dc), in order of dr then dc over -3..3, among the offsets with max(|dr|, |dc|) > 1. `fine_op`: as for fine_src. `parent_src`: as for fine_src, on the parent grid. `parent_op`: as for fine_op, on the parent grid.
All inputs are finite; a program needn't handle non-finite values.
Results may differ from the reference program's by a relative error of at most 0.0022.
Values may be sent and summed in bfloat16 or wider, within the bound.
A program may use at most 128 MiB of HBM per device.

```python
import jax
import jax.numpy as jnp
import numpy as np
from jax import lax

RHS = 4
DF = 512
DP = 2048
OPS = 40
SLOTS = 32
PR = 48
PC = 64
FR = 96
FC = 128


def offset_table():
    pairs = [(first, second) for first in range(-3, 4) for second in range(-3, 4) if max(abs(first), abs(second)) > 1]
    return np.array(pairs, dtype=np.int32)


def build_lists(key, height, across):
    offsets = jnp.asarray(offset_table())
    how_many = offsets.shape[0]
    occ_key, order_key = jax.random.split(key)
    occupied = jax.random.randint(occ_key, (height, across), 0, 10) < 8
    row_at = jnp.arange(height, dtype=jnp.int32)[:, None, None]
    col_at = jnp.arange(across, dtype=jnp.int32)[None, :, None]
    src_row = row_at + offsets[:, 0][None, None, :]
    src_col = col_at + offsets[:, 1][None, None, :]
    inside = (src_row >= 0) & (src_row < height) & (src_col >= 0) & (src_col < across)
    beside = (jnp.abs(src_row // 2 - row_at // 2) <= 1) & (jnp.abs(src_col // 2 - col_at // 2) <= 1)
    safe_row = jnp.clip(src_row, 0, height - 1)
    safe_col = jnp.clip(src_col, 0, across - 1)
    usable = inside & beside & occupied[safe_row, safe_col]
    jitter = jax.random.randint(order_key, (height, across, how_many), 0, 1 << 16) * 64 + jnp.arange(how_many, dtype=jnp.int32)
    ranking = jnp.where(usable, jitter + (1 << 23), jitter)
    _, picked = lax.top_k(ranking, SLOTS)
    picked = picked.astype(jnp.int32)
    chosen = jnp.take_along_axis(usable, picked, axis=2)
    own_box = row_at * across + col_at
    source = jnp.where(chosen, jnp.take_along_axis(safe_row * across + safe_col, picked, axis=2), own_box)
    opcode = jnp.where(chosen, picked, OPS)
    return (source.astype(jnp.int32), opcode.astype(jnp.int32))


def draw_fine_src(key, part):
    return build_lists(jax.random.fold_in(key, 11), FR, FC)[0]


def draw_fine_op(key, part):
    return build_lists(jax.random.fold_in(key, 11), FR, FC)[1]


def draw_parent_src(key, part):
    return build_lists(jax.random.fold_in(key, 23), PR, PC)[0]


def draw_parent_op(key, part):
    return build_lists(jax.random.fold_in(key, 23), PR, PC)[1]


def block_scale(stream_key, dims, cuts, least, high):
    factor_of = 1.0
    for position, parts in cuts:
        steps = jax.random.uniform(jax.random.fold_in(jax.random.fold_in(stream_key, 6), position), (parts,), jnp.float32, least / len(cuts), high / len(cuts))
        factor_of = factor_of * jnp.repeat(jnp.exp(steps), dims[position] // parts).reshape((-1,) + (1,) * (len(dims) - 1 - position))
    return factor_of


def gaussian(stream_key, shape, deviation, most, shards=(), kind=jnp.bfloat16):
    loudness = block_scale(stream_key, shape, shards, -0.22, 0.18) if shards else 1.0
    entries = jax.random.normal(stream_key, shape, jnp.float32) * deviation * loudness
    return jnp.minimum(jnp.maximum(entries, -most), most).astype(kind)


def setup_inputs(seed: int = 0) -> dict:
    splits = jax.random.split(jax.random.key(seed), 10)
    return {
        "fine_out": gaussian(splits[0], (FR, FC, 2, RHS, DF), 1.0, 6.0, ((0, 16), (1, 32))),
        "interp": gaussian(splits[1], (DF, DP), DF ** -0.5, 0.25),
        "child_phase": jnp.clip(jax.random.uniform(splits[2], (4, DP), jnp.float32, -3.140625, 3.140625), -3.140625, 3.140625),
        "fine_ops": gaussian(splits[3], (OPS, 2, DF), 0.2, 1.2, (), jnp.float32),
        "parent_ops": gaussian(splits[4], (OPS, 2, DP), 0.1, 0.6, ((2, 32),), jnp.float32),
        "fine_src": draw_fine_src(jax.random.fold_in(splits[9], 71), 0),
        "fine_op": draw_fine_op(jax.random.fold_in(splits[9], 71), 0),
        "parent_src": draw_parent_src(jax.random.fold_in(splits[9], 71), 0),
        "parent_op": draw_parent_op(jax.random.fold_in(splits[9], 71), 0),
    }


highest = lax.Precision.HIGHEST


def translate(sources, index, opcode, operators):
    kinds = operators.shape[0]

    def add_slot(running, slot_pair):
        where_from, which_op = slot_pair
        pieces = sources[where_from].astype(jnp.float32)
        one_hot = (which_op[:, None] == jnp.arange(kinds, dtype=jnp.int32)[None, :]).astype(jnp.float32)
        factor = jnp.einsum("bo,ocd->bcd", one_hot, operators, precision=highest)
        cos_part = factor[:, 0, None, :]
        sin_part = factor[:, 1, None, :]
        real_part = cos_part * pieces[:, 0] - sin_part * pieces[:, 1]
        imag_part = cos_part * pieces[:, 1] + sin_part * pieces[:, 0]
        return running + jnp.stack([real_part, imag_part], axis=1), None

    start = jnp.zeros((index.shape[0],) + sources.shape[1:], jnp.float32)
    running, _ = lax.scan(add_slot, start, (index.T, opcode.T))
    return running


def reference(fine_out, interp, child_phase, fine_ops, parent_ops, fine_src, fine_op, parent_src, parent_op):
    fine_rows, fine_cols = fine_out.shape[0], fine_out.shape[1]
    par_rows, par_cols = fine_rows // 2, fine_cols // 2
    cosine = jnp.cos(child_phase).reshape(2, 2, DP)[:, None, :, None, :]
    sine_ab = jnp.sin(child_phase).reshape(2, 2, DP)[:, None, :, None, :]
    interp_wide = interp.astype(jnp.float32)

    def aggregate(strip):
        spread = jnp.dot(strip.reshape(-1, DF).astype(jnp.float32), interp_wide, precision=highest)
        spread = spread.reshape(2, par_cols, 2, 2, RHS, DP)
        real_in = spread[:, :, :, 0]
        imag_in = spread[:, :, :, 1]
        real_sum = jnp.sum(cosine * real_in - sine_ab * imag_in, axis=(0, 2))
        imag_sum = jnp.sum(cosine * imag_in + sine_ab * real_in, axis=(0, 2))
        return jnp.stack([real_sum, imag_sum], axis=1).astype(jnp.bfloat16)

    parent_out = lax.map(aggregate, fine_out.reshape(par_rows, 2, fine_cols, 2, RHS, DF))
    parent_flat = parent_out.reshape(par_rows * par_cols, 2, RHS, DP)

    def parent_row(pair):
        return translate(parent_flat, pair[0], pair[1], parent_ops).astype(jnp.bfloat16)

    parent_in = lax.map(parent_row, (parent_src, parent_op))

    def disaggregate(strip):
        wide_strip = strip.astype(jnp.float32)
        real_in = wide_strip[None, :, None, 0]
        imag_in = wide_strip[None, :, None, 1]
        real_child = cosine * real_in + sine_ab * imag_in
        imag_child = cosine * imag_in - sine_ab * real_in
        child_in = jnp.stack([real_child, imag_child], axis=3).astype(jnp.bfloat16)
        child_in = child_in.reshape(-1, DP).astype(jnp.float32)
        back = jnp.dot(child_in, interp_wide.T, precision=highest) * (DF / DP)
        return back.reshape(2, fine_cols, 2, RHS, DF)

    fine_far = lax.map(disaggregate, parent_in).reshape(fine_rows, fine_cols, 2, RHS, DF)
    fine_flat = fine_out.reshape(fine_rows * fine_cols, 2, RHS, DF)

    def fine_row(pair):
        return translate(fine_flat, pair[0], pair[1], fine_ops)

    fine_near = lax.map(fine_row, (fine_src, fine_op))
    return fine_near + fine_far
```

```python
import functools

import jax
import jax.numpy as jnp
from jax import lax
from jax.experimental import pallas as pl
from jax.experimental.pallas import tpu as pltpu
from jax.sharding import PartitionSpec as P

MESH = pl.DeviceIdType.MESH
ZN = 8
OFFSETS = [(a, b) for a in range(-3, 4) for b in range(-3, 4) if max(abs(a), abs(b)) > 1]
OP_ID = {pair: i for i, pair in enumerate(OFFSETS)}


def flip(v):
    turned = pltpu.roll(v, 4, 0)
    top = lax.broadcasted_iota(jnp.int32, v.shape, 0) < 4
    return jnp.where(top, -turned, turned)


def exchange_kernel(x_ref, ops_ref, blk, opsg, ssem, rsem, lsem, ysem, rs, rr, ls, lr, es, er):
    np_, nd = lax.axis_size("patch"), lax.axis_size("dir")
    p, d = lax.axis_index("patch"), lax.axis_index("dir")
    core = lax.rem(d, 2)
    z = lax.rem(d // 2, ZN)
    y = d // (2 * ZN)
    up, down = lax.rem(p + 1, np_), lax.rem(p + np_ - 1, np_)
    other = d + 1 - 2 * core
    outer = lax.rem(d - 1 + 2 * core + nd, nd)
    far = lax.rem(d + 2 * ZN, nd)
    zr, zl = lax.rem(z + 1, ZN), lax.rem(z + ZN - 1, ZN)
    right = y * 2 * ZN + zr * 2 + core
    left = y * 2 * ZN + zl * 2 + core

    barrier = pltpu.get_barrier_semaphore()
    peers = [(up, d), (down, d), (p, other), (p, outer), (p, far), (p, right), (p, left)]
    for peer in peers:
        pl.semaphore_signal(barrier, inc=1, device_id=peer, device_id_type=MESH)
    pl.semaphore_wait(barrier, len(peers))

    def send(src, dst, s, r, peer):
        return pltpu.make_async_remote_copy(
            src_ref=src, dst_ref=dst, send_sem=s, recv_sem=r, device_id=peer, device_id_type=MESH
        )

    own_ops = pltpu.make_async_copy(ops_ref, opsg.at[core, z, y], lsem.at[0])
    own_ops.start()
    own_blk = pltpu.make_async_copy(x_ref, blk.at[1, 0], lsem.at[1])
    own_blk.start()
    to_up = send(x_ref, blk.at[0, 0], ssem.at[0], rsem.at[0], (up, d))
    to_down = send(x_ref, blk.at[2, 0], ssem.at[1], rsem.at[1], (down, d))
    to_outer = send(x_ref, blk.at[1, 2], ssem.at[2], rsem.at[2], (p, outer))
    to_other = send(x_ref, blk.at[1, 1], ssem.at[3], rsem.at[3], (p, other))
    to_far = send(ops_ref, opsg.at[core, z, y], ysem.at[0], ysem.at[1], (p, far))
    to_far.start()
    to_outer.start()
    to_up.start()
    to_down.start()
    to_other.start()

    up_other = send(blk.at[0, 0], blk.at[0, 1], ssem.at[4], rsem.at[4], (p, other))
    down_other = send(blk.at[2, 0], blk.at[2, 1], ssem.at[5], rsem.at[5], (p, other))
    outer_up = send(blk.at[1, 2], blk.at[0, 2], ssem.at[6], rsem.at[6], (up, d))
    outer_down = send(blk.at[1, 2], blk.at[2, 2], ssem.at[7], rsem.at[7], (down, d))

    def slot(k):
        return opsg.at[core, lax.rem(z + k + ZN, ZN)]

    def go_right(step):
        ref = slot(-step)
        return send(ref, ref, rs.at[step], rr.at[step], (p, right))

    def go_left(step):
        ref = slot(step)
        return send(ref, ref, ls.at[step], lr.at[step], (p, left))

    def go_other(k):
        ref = slot(k)
        return send(ref, ref, es.at[k + 4], er.at[k + 4], (p, other))

    to_up.wait_recv()
    up_other.start()
    to_down.wait_recv()
    down_other.start()
    cross = jnp.logical_or(jnp.logical_and(core == 0, z == 0), jnp.logical_and(core == 1, z == ZN - 1))

    @pl.when(jnp.logical_not(cross))
    def _():
        to_outer.wait_recv()
        outer_up.start()
        outer_down.start()

    own_ops.wait()
    to_far.wait()
    go_right(0).start()
    go_left(0).start()
    go_other(0).start()
    for step in range(4):
        go_right(step).wait_recv()
        if step < 3:
            go_right(step + 1).start()
        go_other(-step - 1).start()
        if step < 3:
            go_left(step).wait_recv()
            if step < 2:
                go_left(step + 1).start()
            go_other(step + 1).start()

    @pl.when(cross)
    def _():
        to_outer.wait_recv()
        outer_up.start()
        outer_down.start()

    for copy in (to_other, up_other, down_other, outer_up, outer_down):
        copy.wait_recv()
    for k in range(-4, 4):
        go_other(k).wait()
    own_blk.wait()
    for copy in (to_up, to_down, to_outer, to_other, up_other, down_other, outer_up, outer_down):
        copy.wait_send()
    for step in range(4):
        go_right(step).wait_send()
        if step < 3:
            go_left(step).wait_send()


def aggregate(block, interp, cosine, sine, parents, row, col):
    def chunk(n, carry):
        lanes = pl.ds(pl.multiple_of(n * 256, 256), 256)
        spread = jnp.dot(block, interp[:, lanes], preferred_element_type=jnp.float32)
        cos_at = [cosine[pl.ds(k, 1), lanes] for k in range(4)]
        sin_at = [sine[pl.ds(k, 1), lanes] for k in range(4)]
        for pr in range(3):
            for pc in range(2):
                first = second = None
                for k in range(4):
                    box = (2 * pr + k // 2) * 4 + 2 * pc + k % 2
                    part = spread[box * 8 : box * 8 + 8]
                    a, b = cos_at[k] * part, sin_at[k] * part
                    first = a if first is None else first + a
                    second = b if second is None else second + b
                value = first + flip(second)
                parents[row + pr, col + pc, :, lanes] = value.astype(jnp.bfloat16).astype(jnp.float32)
        return carry

    lax.fori_loop(0, interp.shape[1] // 256, chunk, 0)


def widen(block, window, row0, rows, row_at, col0, cols, col_at):
    for r in range(rows):
        for c in range(0, cols, 2):
            start = (row0 + r) * 4 + col0 + c
            pair = block[start * 8 : start * 8 + 16].astype(jnp.float32)
            window[row_at + r, col_at + c] = pair[:8]
            window[row_at + r, col_at + c + 1] = pair[8:]


def near_field(window, ops, present, near):
    def one(step, carry):
        pair, lane = step // 4, lax.rem(step, 4)
        lanes = pl.ds(pl.multiple_of(lane * 128, 128), 128)
        targets = [(kr, c) for kr in range(2) for c in range(4)]
        first = {t: None for t in targets}
        second = {t: None for t in targets}
        for op, (dr, dc) in enumerate(OFFSETS):
            used = [
                (kr, c)
                for kr, c in targets
                if -2 - kr <= dr <= 3 - kr and -2 - c % 2 <= dc <= 3 - c % 2
            ]
            if not used:
                continue
            cos_part = ops[op, pl.ds(0, 1), lanes]
            sin_part = ops[op, pl.ds(1, 1), lanes]
            for t in used:
                kr, c = t
                source = window[2 * pair + 2 + kr + dr, 2 + c + dc, :, lanes]
                source = source * present[(2 * pair + kr) * 4 + c, op]
                a, b = cos_part * source, sin_part * source
                first[t] = a if first[t] is None else first[t] + a
                second[t] = b if second[t] is None else second[t] + b
        for t in targets:
            near[(2 * pair + t[0]) * 4 + t[1], :, lanes] = first[t] + flip(second[t])
        return carry

    lax.fori_loop(0, 12, one, 0)


def far_translate(parents, opsg, present, parent_in, cos_ops, sin_ops, odd):
    def one(chunk, carry):
        lanes = pl.ds(pl.multiple_of(chunk * 128, 128), 128)
        y, z = chunk // ZN, lax.rem(chunk, ZN)
        even, uneven = opsg[0, z, y], opsg[1, z, y]
        low = lax.broadcasted_iota(jnp.int32, even.shape, 1) < 64
        cos_ops[...] = jnp.where(low, even, pltpu.roll(uneven, 64, 1))
        sin_ops[...] = jnp.where(low, pltpu.roll(even, 64, 1), uneven)
        for pc in range(2):
            targets = range(3)
            first = {t: None for t in targets}
            second = {t: None for t in targets}
            for dc in range(-2 - pc, 4 - pc):
                if abs(dc) >= 2:
                    steps = [(t, t) for t in range(6)]
                else:
                    steps = [(0, 0), (4, 1), (5, 5)]
                for rows, parity in (((0, 2), odd), ((1,), 1 - odd)):
                    for even_step, odd_step in steps:
                        dr0, dr1 = even_step - 2, odd_step - 3
                        id0, id1 = OP_ID[(dr0, dc)], OP_ID[(dr1, dc)]
                        op = id0 + parity * (id1 - id0)
                        shift = dr0 + parity * (dr1 - dr0)
                        cos_part = cos_ops[pl.ds(op, 1), :]
                        sin_part = sin_ops[pl.ds(op, 1), :]
                        for t in rows:
                            source = parents[3 + t + shift, 2 + pc + dc, :, lanes]
                            source = source * present[t * 2 + pc, op]
                            a, b = cos_part * source, sin_part * source
                            first[t] = a if first[t] is None else first[t] + a
                            second[t] = b if second[t] is None else second[t] + b
            for t in targets:
                value = first[t] + flip(second[t])
                parent_in[t * 2 + pc, :, lanes] = value.astype(jnp.bfloat16).astype(jnp.float32)
        return carry

    lax.fori_loop(0, parent_in.shape[-1] // 128, one, 0)


def disaggregate(parent_in, cosine, sine, child):
    def one(n, carry):
        lanes = pl.ds(pl.multiple_of(n * 256, 256), 256)
        cos_at = [cosine[pl.ds(k, 1), lanes] for k in range(4)]
        sin_at = [sine[pl.ds(k, 1), lanes] for k in range(4)]
        for pr in range(3):
            for pc in range(2):
                value = parent_in[pr * 2 + pc, :, lanes]
                turned = flip(value)
                for kr in range(2):
                    both = [cos_at[2 * kr + kc] * value - sin_at[2 * kr + kc] * turned for kc in range(2)]
                    box = (2 * pr + kr) * 4 + 2 * pc
                    child[box * 8 : box * 8 + 16, lanes] = jnp.concatenate(both, axis=0).astype(jnp.bfloat16)
        return carry

    lax.fori_loop(0, child.shape[1] // 256, one, 0)


def compute_kernel(
    fine_on, par_on, blk, opsg, interp, phase, fine_ops, out,
    parents, window, near, parent_in, child, cosine, sine, cos_ops, sin_ops,
):
    p, d = lax.axis_index("patch"), lax.axis_index("dir")
    core = lax.rem(d, 2)
    odd = lax.rem(p, 2)
    cosine[...] = jnp.cos(phase[...])
    sine[...] = jnp.sin(phase[...])
    col_of = [2, 4 - 4 * core, 4 * core]

    for i, (row0, rows, row_at) in enumerate(((4, 2, 0), (0, 6, 2), (0, 2, 8))):
        widen(blk.at[i, 0], window, row0, rows, row_at, 0, 4, 2)

        @pl.when(core == 0)
        def _(i=i, row0=row0, rows=rows, row_at=row_at):
            widen(blk.at[i, 1], window, row0, rows, row_at, 0, 2, 6)
            widen(blk.at[i, 2], window, row0, rows, row_at, 2, 2, 0)

        @pl.when(core == 1)
        def _(i=i, row0=row0, rows=rows, row_at=row_at):
            widen(blk.at[i, 1], window, row0, rows, row_at, 2, 2, 0)
            widen(blk.at[i, 2], window, row0, rows, row_at, 0, 2, 6)

    near_field(window, fine_ops, fine_on, near)
    for q in range(3):

        def strip(i, carry, q=q):
            aggregate(blk[i, q], interp, cosine, sine, parents, 3 * i, col_of[q])
            return carry

        lax.fori_loop(0, 3, strip, 0)
    far_translate(parents, opsg, par_on, parent_in, cos_ops, sin_ops, odd)
    disaggregate(parent_in, cosine, sine, child)
    back = lax.dot_general(
        child[...], interp[...], (((1,), (1,)), ((), ())), preferred_element_type=jnp.float32
    )
    scale = interp.shape[0] / interp.shape[1]
    for r in range(6):
        for c in range(4):
            box = r * 4 + c
            total = near[box] + back[box * 8 : box * 8 + 8] * scale
            out[r, c, 0] = total[:4]
            out[r, c, 1] = total[4:]


def per_device(
    fine_out, interp, child_phase, fine_ops, parent_ops, fine_src, fine_op, parent_src, parent_op
):
    dir_at = lax.axis_index("dir")
    dp = interp.shape[1]
    kinds = fine_ops.shape[0]

    def present(opcode, width):
        mine = lax.dynamic_slice_in_dim(opcode, dir_at * width, width, 1)
        hits = mine.reshape(-1, 1, opcode.shape[-1]) == jnp.arange(kinds, dtype=jnp.int32)[None, :, None]
        return jnp.any(hits, axis=2).astype(jnp.float32)

    fine_on, par_on = present(fine_op, 4), present(parent_op, 2)
    x = fine_out.reshape(192, 512)
    ops = parent_ops.reshape(kinds, 128)
    dma = pltpu.SemaphoreType.DMA
    hbm = pl.BlockSpec(memory_space=pl.ANY)
    blk, opsg = pl.pallas_call(
        exchange_kernel,
        out_shape=(
            jax.ShapeDtypeStruct((3, 3, 192, 512), jnp.bfloat16),
            jax.ShapeDtypeStruct((2, ZN, 2, kinds, 128), jnp.float32),
        ),
        in_specs=[hbm, hbm],
        out_specs=(hbm, hbm),
        scratch_shapes=[
            dma((8,)), dma((8,)), dma((2,)), dma((2,)), dma((4,)), dma((4,)), dma((3,)), dma((3,)), dma((8,)), dma((8,)),
        ],
        compiler_params=pltpu.CompilerParams(collective_id=0, has_side_effects=True),
        name="exchange",
    )(x, ops)
    vmem = pl.BlockSpec(memory_space=pltpu.VMEM)
    smem = pl.BlockSpec(memory_space=pltpu.SMEM)
    f32 = jnp.float32
    return pl.pallas_call(
        compute_kernel,
        out_shape=jax.ShapeDtypeStruct((6, 4, 2, 4, 512), f32),
        in_specs=[smem, smem, vmem, vmem, vmem, vmem, vmem],
        out_specs=vmem,
        scratch_shapes=[
            pltpu.VMEM((9, 6, 8, dp), f32),
            pltpu.VMEM((10, 8, 8, 512), f32),
            pltpu.VMEM((24, 8, 512), f32),
            pltpu.VMEM((6, 8, dp), f32),
            pltpu.VMEM((192, dp), jnp.bfloat16),
            pltpu.VMEM((4, dp), f32),
            pltpu.VMEM((4, dp), f32),
            pltpu.VMEM((kinds, 128), f32),
            pltpu.VMEM((kinds, 128), f32),
        ],
        compiler_params=pltpu.CompilerParams(vmem_limit_bytes=40 * 1024 * 1024),
        name="translate",
    )(fine_on, par_on, blk, opsg, interp, child_phase, fine_ops)


def solution(mesh):
    in_specs = (
        P("patch", "dir", None, None, None),
        P(),
        P(),
        P(),
        P(None, None, "dir"),
        P("patch", None, None),
        P("patch", None, None),
        P("patch", None, None),
        P("patch", None, None),
    )
    out_specs = P("patch", "dir", None, None, None)
    return jax.shard_map(
        per_device, mesh=mesh, in_specs=in_specs, out_specs=out_specs, check_vma=False
    )
```

```python
import jax
import jax.numpy as jnp
from jax import lax
from jax.experimental import pallas as pl
from jax.experimental.pallas import tpu as pltpu
from jax.sharding import PartitionSpec as P

MESH = pl.DeviceIdType.MESH
ZN = 8
OFFSETS = [(a, b) for a in range(-3, 4) for b in range(-3, 4) if max(abs(a), abs(b)) > 1]
F32, BF16 = jnp.float32, jnp.bfloat16


def flip(v):
    turned = pltpu.roll(v, 4, 0)
    top = lax.broadcasted_iota(jnp.int32, v.shape, 0) < 4
    return jnp.where(top, -turned, turned)


def row_of(ref, r, lanes):
    return ref[pl.ds(r, 1), lanes]


def aggregate(blk, first_slot, count, interp, cosine, sine, parents, places):
    def chunk(n, carry):
        lanes = pl.ds(pl.multiple_of(n * 256, 256), 256)
        rows = blk[pl.ds(first_slot * 192, count * 192), :]
        spread = jnp.dot(rows, interp[:, lanes], preferred_element_type=F32)
        cos_at = [row_of(cosine, k, lanes) for k in range(4)]
        sin_at = [row_of(sine, k, lanes) for k in range(4)]
        for which, (row, col) in enumerate(places):
            for pr in range(3):
                for pc in range(2):
                    first = second = None
                    for k in range(4):
                        start = which * 192 + ((2 * pr + k // 2) * 4 + 2 * pc + k % 2) * 8
                        part = spread[start : start + 8]
                        a, b = cos_at[k] * part, sin_at[k] * part
                        first = a if first is None else first + a
                        second = b if second is None else second + b
                    value = first + flip(second)
                    parents[row + pr, col + pc, :, lanes] = value.astype(BF16).astype(F32)
        return carry

    lax.fori_loop(0, interp.shape[1] // 256, chunk, 0, unroll=2)


def widen(blk, slot, window, row0, rows, row_at, col0, cols, col_at):
    for r in range(rows):
        for c in range(0, cols, 2):
            start = slot * 192 + ((row0 + r) * 4 + col0 + c) * 8
            pair = blk[start : start + 16, :].astype(F32)
            window[row_at + r, col_at + c] = pair[:8]
            window[row_at + r, col_at + c + 1] = pair[8:]


def near_field(window, ops, present, near, core, late):
    def is_late(col):
        return col < 2 if core == 0 else col >= 6

    def one(step, carry):
        pair, lane = step // 4, lax.rem(step, 4)
        lanes = pl.ds(pl.multiple_of(lane * 128, 128), 128)
        first, second = {}, {}
        for op, (dr, dc) in enumerate(OFFSETS):
            used = [
                (kr, c)
                for kr in range(2)
                for c in range(4)
                if -2 - kr <= dr <= 3 - kr and -2 - c % 2 <= dc <= 3 - c % 2 and is_late(2 + c + dc) == late
            ]
            if not used:
                continue
            cos_part = ops[op, pl.ds(0, 1), lanes]
            sin_part = ops[op, pl.ds(1, 1), lanes]
            for t in used:
                kr, c = t
                source = window[2 * pair + 2 + kr + dr, 2 + c + dc, :, lanes]
                source = source * present[(2 * pair + kr) * 4 + c, op]
                a, b = cos_part * source, sin_part * source
                first[t] = first[t] + a if t in first else a
                second[t] = second[t] + b if t in second else b
        for t in first:
            value = first[t] + flip(second[t])
            box = (2 * pair + t[0]) * 4 + t[1]
            near[box, :, lanes] = near[box, :, lanes] + value if late else value
        return carry

    lax.fori_loop(0, 12, one, 0)


def far_sums(parents, cos_ops, sin_ops, present, lanes, core, odd, late):
    def is_late(col):
        return col < 2 if core == 0 else col >= 4

    first, second = {}, {}
    for op, (dr, dc) in enumerate(OFFSETS):
        used = [
            (pr, pc)
            for pr in range(3)
            for pc in range(2)
            if -2 - (odd + pr) % 2 <= dr <= 3 - (odd + pr) % 2
            and -2 - pc <= dc <= 3 - pc
            and is_late(2 + pc + dc) == late
        ]
        if not used:
            continue
        cos_part = row_of(cos_ops, op, lanes)
        sin_part = row_of(sin_ops, op, lanes)
        for t in used:
            pr, pc = t
            source = parents[3 + pr + dr, 2 + pc + dc, :, lanes]
            source = source * present[24 + pr * 2 + pc, op]
            a, b = cos_part * source, sin_part * source
            first[t] = first[t] + a if t in first else a
            second[t] = second[t] + b if t in second else b
    return {t: first[t] + flip(second[t]) for t in first}


def far_early(parents, cos_ops, sin_ops, present, parent_in, core, odd):
    def one(n, carry):
        lanes = pl.ds(pl.multiple_of(n * 256, 256), 256)
        sums = far_sums(parents, cos_ops, sin_ops, present, lanes, core, odd, False)
        for (pr, pc), value in sums.items():
            parent_in[pr * 2 + pc, :, lanes] = value
        return carry

    lax.fori_loop(0, parent_in.shape[-1] // 256, one, 0)


def far_late(parents, cos_ops, sin_ops, present, parent_in, cosine, sine, child, core, odd):
    def one(n, carry):
        lanes = pl.ds(pl.multiple_of(n * 256, 256), 256)
        sums = far_sums(parents, cos_ops, sin_ops, present, lanes, core, odd, True)
        for pr in range(3):
            for pc in range(2):
                value = parent_in[pr * 2 + pc, :, lanes] + sums[(pr, pc)]
                value = value.astype(BF16).astype(F32)
                turned = flip(value)
                for kr in range(2):
                    both = [
                        row_of(cosine, 2 * kr + kc, lanes) * value - row_of(sine, 2 * kr + kc, lanes) * turned
                        for kc in range(2)
                    ]
                    box = (2 * pr + kr) * 4 + 2 * pc
                    child[box * 8 : box * 8 + 16, lanes] = jnp.concatenate(both, axis=0).astype(BF16)
        return carry

    lax.fori_loop(0, parent_in.shape[-1] // 256, one, 0)


def kernel(
    x_hbm, ops_hbm, interp_hbm, phase_hbm, fine_ops_hbm, fine_list_hbm, par_list_hbm, out,
    blk, opsg, x_raw, ops_raw, interp, phase, fine_ops, fine_list, par_list, on_vec, on,
    parents, window, near, parent_in, child, cosine, sine, cos_ops, sin_ops,
    ssem, rsem, lsem, ysem, zs, zr, es, er,
):
    np_, nd = lax.axis_size("patch"), lax.axis_size("dir")
    p, d = lax.axis_index("patch"), lax.axis_index("dir")
    core, z, y = lax.rem(d, 2), lax.rem(d // 2, ZN), d // (2 * ZN)
    odd = lax.rem(p, 2)
    up, down = lax.rem(p + 1, np_), lax.rem(p + np_ - 1, np_)
    other = d + 1 - 2 * core
    outer = lax.rem(d - 1 + 2 * core + nd, nd)
    far = lax.rem(d + 2 * ZN, nd)
    has_up, has_down = p < np_ - 1, p > 0
    has_outer = jnp.logical_and(d > 0, d < nd - 1)
    z_peer = [(p, y * 2 * ZN + lax.rem(z + k, ZN) * 2 + core) for k in range(ZN)]
    barrier = pltpu.get_barrier_semaphore()

    def greet(peer):
        pl.semaphore_signal(barrier, inc=1, device_id=peer, device_id_type=MESH)

    for peer in [(p, other), (p, far)] + z_peer[1:]:
        greet(peer)
    pl.when(has_up)(lambda: greet((up, d)))
    pl.when(has_down)(lambda: greet((down, d)))
    pl.when(has_outer)(lambda: greet((p, outer)))

    pairs = [
        (x_hbm, x_raw), (ops_hbm, ops_raw), (phase_hbm, phase), (interp_hbm, interp),
        (fine_list_hbm, fine_list), (par_list_hbm, par_list), (fine_ops_hbm, fine_ops),
    ]
    loads = [pltpu.make_async_copy(a, b, lsem.at[i]) for i, (a, b) in enumerate(pairs)]
    for load in loads:
        load.start()
    loads[0].wait()
    for r in range(6):
        for c in range(0, 4, 2):
            parts = [x_raw[r, c + i // 2, i % 2].astype(F32) for i in range(4)]
            blk[(r * 4 + c) * 8 : (r * 4 + c) * 8 + 16, :] = jnp.concatenate(parts, axis=0).astype(BF16)
    loads[1].wait()
    opsg[core, z, y] = jnp.concatenate([ops_raw[:, 0, :], ops_raw[:, 1, :]], axis=1)

    one = lambda flag: flag.astype(jnp.int32)
    pl.semaphore_wait(barrier, 2 + ZN - 1 + one(has_up) + one(has_down) + one(has_outer))

    def at(slot, count=1):
        return blk.at[pl.ds(slot * 192, count * 192)]

    def send(src, dst, s, r, peer):
        return pltpu.make_async_remote_copy(
            src_ref=src, dst_ref=dst, send_sem=s, recv_sem=r, device_id=peer, device_id_type=MESH
        )

    def block(src, dst, peer):
        return send(at(src), at(dst), ssem.at[dst - 1], rsem.at[dst - 1], peer)

    to_other, to_outer = block(0, 1, (p, other)), block(0, 2, (p, outer))
    to_up, to_down = block(0, 3, (up, d)), block(0, 4, (down, d))
    up_other, down_other = block(3, 5, (p, other)), block(4, 6, (p, other))
    outer_up, outer_down = block(2, 7, (up, d)), block(2, 8, (down, d))
    to_far = send(opsg.at[core, z, y], opsg.at[core, z, y], ysem.at[0], ysem.at[1], (p, far))

    to_far.start()
    pl.when(has_outer)(lambda: to_outer.start())
    pl.when(has_up)(lambda: to_up.start())
    pl.when(has_down)(lambda: to_down.start())
    to_other.start()

    def z_send(k):
        ref = opsg.at[core, z]
        return send(ref, ref, zs.at[k], zr.at[k], z_peer[k])

    def z_arrival(k):
        ref = opsg.at[core, lax.rem(z - k + ZN, ZN)]
        return send(ref, ref, zs.at[k], zr.at[k], z_peer[k])

    def pass_on(k):
        ref = opsg.at[core, lax.rem(z - k + ZN, ZN)]
        return send(ref, ref, es.at[k], er.at[k], (p, other))

    def clear(slots):
        for slot in slots:
            blk[slot * 192 : (slot + 1) * 192, :] = jnp.zeros((192, 512), BF16)

    pl.when(jnp.logical_not(has_down))(lambda: clear((3, 5, 7)))
    pl.when(jnp.logical_not(has_up))(lambda: clear((4, 6, 8)))
    pl.when(jnp.logical_and(jnp.logical_not(has_outer), has_down))(lambda: clear((7,)))
    pl.when(jnp.logical_and(jnp.logical_not(has_outer), has_up))(lambda: clear((8,)))
    pl.when(jnp.logical_not(has_outer))(lambda: clear((2,)))

    loads[2].wait()
    cosine[...] = jnp.cos(phase[...])
    sine[...] = jnp.sin(phase[...])
    loads[4].wait()
    loads[5].wait()
    kind = lax.broadcasted_iota(jnp.int32, (32, 128), 1)
    for r in range(6):
        lists = fine_list[r]
        for c in range(4):
            mine = jnp.sum(jnp.where(kind == 4 * d + c, lists, 0), axis=1, keepdims=True)
            on_vec[r * 4 + c : r * 4 + c + 1, :] = jnp.sum(jnp.where(mine == kind, 1.0, 0.0), axis=0, keepdims=True)
    kind64 = lax.broadcasted_iota(jnp.int32, (32, 64), 1)
    for r in range(3):
        lists = par_list[r]
        for c in range(2):
            mine = jnp.sum(jnp.where(kind64 == 2 * d + c, lists, 0), axis=1, keepdims=True)
            row = 24 + r * 2 + c
            on_vec[row : row + 1, :] = jnp.sum(jnp.where(mine == kind, 1.0, 0.0), axis=0, keepdims=True)
    to_smem = pltpu.make_async_copy(on_vec, on, lsem.at[7])
    to_smem.start()

    other_col, outer_col = 4 - 4 * core, 4 * core
    loads[3].wait()
    to_other.wait_recv()
    aggregate(blk, 0, 2, interp, cosine, sine, parents, [(3, 2), (3, other_col)])

    to_far.wait()
    for k in (1, 7, 2, 6, 3, 5, 4):
        z_send(k).start()
    pass_on(0).start()

    @pl.when(has_outer)
    def _():
        to_outer.wait_recv()
        pl.when(has_up)(lambda: outer_up.start())
        pl.when(has_down)(lambda: outer_down.start())

    @pl.when(has_down)
    def _():
        to_up.wait_recv()
        up_other.start()

    @pl.when(has_up)
    def _():
        to_down.wait_recv()
        down_other.start()

    aggregate(blk, 2, 3, interp, cosine, sine, parents, [(3, outer_col), (0, 2), (6, 2)])
    for k in (1, 7, 2, 6, 3, 5, 4):
        z_arrival(k).wait_recv()
        pass_on(k).start()
    pl.when(has_down)(lambda: up_other.wait_recv())
    pl.when(has_up)(lambda: down_other.wait_recv())
    aggregate(blk, 5, 2, interp, cosine, sine, parents, [(0, other_col), (6, other_col)])

    def widen_strips(slots, row0, rows, row_at, col0, cols, col_at):
        for slot, a, b, c in zip(slots, row0, rows, row_at):
            widen(blk, slot, window, a, b, c, col0, cols, col_at)

    widen_strips((0, 3, 4), (0, 4, 0), (6, 2, 2), (2, 0, 8), 0, 4, 2)
    pl.when(core == 0)(lambda: widen_strips((1, 5, 6), (0, 4, 0), (6, 2, 2), (2, 0, 8), 0, 2, 6))
    pl.when(core == 1)(lambda: widen_strips((1, 5, 6), (0, 4, 0), (6, 2, 2), (2, 0, 8), 2, 2, 0))
    to_smem.wait()
    loads[6].wait()
    for which in range(2):
        pl.when(core == which)(lambda which=which: near_field(window, fine_ops, on, near, which, False))

    for k in range(ZN):
        pass_on(k).wait_recv()

    def gather_ops(chunk, carry):
        lanes = pl.ds(pl.multiple_of(chunk * 128, 128), 128)
        even, uneven = (opsg[i, lax.rem(chunk, ZN), chunk // ZN] for i in range(2))
        low = lax.broadcasted_iota(jnp.int32, even.shape, 1) < 64
        cos_ops[:, lanes] = jnp.where(low, even, pltpu.roll(uneven, 64, 1))
        sin_ops[:, lanes] = jnp.where(low, pltpu.roll(even, 64, 1), uneven)
        return carry

    lax.fori_loop(0, 2 * ZN, gather_ops, 0)
    variants = [(a, b) for a in range(2) for b in range(2)]
    for a, b in variants:
        pl.when(jnp.logical_and(core == a, odd == b))(
            lambda a=a, b=b: far_early(parents, cos_ops, sin_ops, on, parent_in, a, b)
        )

    pl.when(jnp.logical_and(has_outer, has_down))(lambda: outer_up.wait_recv())
    pl.when(jnp.logical_and(has_outer, has_up))(lambda: outer_down.wait_recv())
    aggregate(blk, 7, 2, interp, cosine, sine, parents, [(0, outer_col), (6, outer_col)])
    for a, b in variants:
        pl.when(jnp.logical_and(core == a, odd == b))(
            lambda a=a, b=b: far_late(parents, cos_ops, sin_ops, on, parent_in, cosine, sine, child, a, b)
        )
    pl.when(core == 0)(lambda: widen_strips((2, 7, 8), (0, 4, 0), (6, 2, 2), (2, 0, 8), 2, 2, 0))
    pl.when(core == 1)(lambda: widen_strips((2, 7, 8), (0, 4, 0), (6, 2, 2), (2, 0, 8), 0, 2, 6))
    for which in range(2):
        pl.when(core == which)(lambda which=which: near_field(window, fine_ops, on, near, which, True))
    back = lax.dot_general(child[...], interp[...], (((1,), (1,)), ((), ())), preferred_element_type=F32)
    scale = interp.shape[0] / interp.shape[1]
    for r in range(6):
        for c in range(4):
            box = r * 4 + c
            total = near[box] + back[box * 8 : box * 8 + 8] * scale
            out[r, c, 0] = total[:4]
            out[r, c, 1] = total[4:]

    to_other.wait_send()
    pl.when(has_outer)(lambda: to_outer.wait_send())
    pl.when(has_up)(lambda: to_up.wait_send())
    pl.when(has_down)(lambda: to_down.wait_send())
    pl.when(has_down)(lambda: up_other.wait_send())
    pl.when(has_up)(lambda: down_other.wait_send())
    pl.when(jnp.logical_and(has_outer, has_up))(lambda: outer_up.wait_send())
    pl.when(jnp.logical_and(has_outer, has_down))(lambda: outer_down.wait_send())
    for k in range(1, ZN):
        z_send(k).wait_send()
    for k in range(ZN):
        pass_on(k).wait_send()


def per_device(
    fine_out, interp, child_phase, fine_ops, parent_ops, fine_src, fine_op, parent_src, parent_op
):
    dp = interp.shape[1]
    kinds = fine_ops.shape[0]
    dma = pltpu.SemaphoreType.DMA
    hbm = pl.BlockSpec(memory_space=pl.ANY)
    vmem = pltpu.VMEM
    fine_list, par_list = (jnp.transpose(v, (0, 2, 1)) for v in (fine_op, parent_op))
    return pl.pallas_call(
        kernel,
        out_shape=jax.ShapeDtypeStruct(fine_out.shape, F32),
        in_specs=[hbm] * 7,
        out_specs=pl.BlockSpec(memory_space=pltpu.VMEM),
        scratch_shapes=[
            vmem((9 * 192, 512), BF16),
            vmem((2, ZN, 2, kinds, 128), F32),
            vmem(fine_out.shape, BF16),
            vmem(parent_ops.shape, F32),
            vmem(interp.shape, BF16),
            vmem((4, dp), F32),
            vmem(fine_ops.shape, F32),
            vmem(fine_list.shape, jnp.int32),
            vmem(par_list.shape, jnp.int32),
            vmem((32, 128), F32),
            pltpu.SMEM((32, 128), F32),
            vmem((9, 6, 8, dp), F32),
            vmem((10, 8, 8, 512), F32),
            vmem((24, 8, 512), F32),
            vmem((6, 8, dp), F32),
            vmem((192, dp), BF16),
            vmem((4, dp), F32),
            vmem((4, dp), F32),
            vmem((kinds, dp), F32),
            vmem((kinds, dp), F32),
            dma((8,)), dma((8,)), dma((8,)), dma((2,)), dma((ZN,)), dma((ZN,)), dma((ZN,)), dma((ZN,)),
        ],
        compiler_params=pltpu.CompilerParams(
            collective_id=0, has_side_effects=True, vmem_limit_bytes=56 * 1024 * 1024
        ),
        name="fmm",
    )(fine_out, parent_ops, interp, child_phase, fine_ops, fine_list, par_list)


def solution(mesh):
    in_specs = (
        P("patch", "dir", None, None, None),
        P(),
        P(),
        P(),
        P(None, None, "dir"),
        P("patch", None, None),
        P("patch", None, None),
        P("patch", None, None),
        P("patch", None, None),
    )
    out_specs = P("patch", "dir", None, None, None)
    return jax.shard_map(
        per_device, mesh=mesh, in_specs=in_specs, out_specs=out_specs, check_vma=False
    )
```

```python
import jax
import jax.numpy as jnp
from jax import lax
from jax.experimental import pallas as pl
from jax.experimental.pallas import tpu as pltpu
from jax.sharding import PartitionSpec as P

MESH = pl.DeviceIdType.MESH
ZN = 8
OFFSETS = [(a, b) for a in range(-3, 4) for b in range(-3, 4) if max(abs(a), abs(b)) > 1]
F32, BF16 = jnp.float32, jnp.bfloat16


def flip(v):
    turned = pltpu.roll(v, 4, 0)
    top = lax.broadcasted_iota(jnp.int32, v.shape, 0) < 4
    return jnp.where(top, -turned, turned)


def row_of(ref, r, lanes):
    return ref[pl.ds(r, 1), lanes]


def aggregate(x, interp, cosine, sine, packed, parents):
    rows = x.reshape(192, 512)

    def chunk(n, carry):
        lanes = pl.ds(pl.multiple_of(n * 256, 256), 256)
        spread = jnp.dot(rows, interp[:, lanes], preferred_element_type=F32)
        cos_at = [row_of(cosine, k, lanes) for k in range(4)]
        sin_at = [row_of(sine, k, lanes) for k in range(4)]
        for pr in range(3):
            pair = []
            for pc in range(2):
                first = second = None
                for k in range(4):
                    start = ((2 * pr + k // 2) * 4 + 2 * pc + k % 2) * 8
                    part = spread[start : start + 8]
                    a, b = cos_at[k] * part, sin_at[k] * part
                    first = a if first is None else first + a
                    second = b if second is None else second + b
                pair.append(first + flip(second))
            rounded = jnp.concatenate(pair, axis=0).astype(BF16)
            packed[pr * 16 : pr * 16 + 16, lanes] = rounded
            wide = rounded.astype(F32)
            parents[3 + pr, 2, :, lanes] = wide[:8]
            parents[3 + pr, 3, :, lanes] = wide[8:]
        return carry

    lax.fori_loop(0, interp.shape[1] // 256, chunk, 0, unroll=2)


def place(packed, slot, parents, row, col):
    for pr in range(3):
        wide = packed[slot * 48 + pr * 16 : slot * 48 + pr * 16 + 16, :].astype(F32)
        parents[row + pr, col] = wide[:8]
        parents[row + pr, col + 1] = wide[8:]


def widen(strip, window, rows, col_at):
    for r in rows:
        pair = strip(r).astype(F32)
        window[r, col_at] = pair[:8]
        window[r, col_at + 1] = pair[8:]


def near_field(window, ops, present, near, core, late, start, stop):
    def is_late(col):
        return col < 2 if core == 0 else col >= 6

    def one(step, carry):
        pair, lane = step // 4, lax.rem(step, 4)
        lanes = pl.ds(pl.multiple_of(lane * 128, 128), 128)
        first, second = {}, {}
        for op, (dr, dc) in enumerate(OFFSETS):
            used = [
                (kr, c)
                for kr in range(2)
                for c in range(4)
                if -2 - kr <= dr <= 3 - kr and -2 - c % 2 <= dc <= 3 - c % 2 and is_late(2 + c + dc) == late
            ]
            if not used:
                continue
            cos_part = ops[op, pl.ds(0, 1), lanes]
            sin_part = ops[op, pl.ds(1, 1), lanes]
            for t in used:
                kr, c = t
                source = window[2 * pair + 2 + kr + dr, 2 + c + dc, :, lanes]
                source = source * present[(2 * pair + kr) * 4 + c, op]
                a, b = cos_part * source, sin_part * source
                first[t] = first[t] + a if t in first else a
                second[t] = second[t] + b if t in second else b
        for t in first:
            value = first[t] + flip(second[t])
            box = (2 * pair + t[0]) * 4 + t[1]
            near[box, :, lanes] = near[box, :, lanes] + value if late else value
        return carry

    lax.fori_loop(start, stop, one, 0)


def far_sums(parents, cos_ops, sin_ops, present, lanes, core, odd, late):
    def is_late(col):
        return col < 2 if core == 0 else col >= 4

    first, second = {}, {}
    for op, (dr, dc) in enumerate(OFFSETS):
        used = [
            (pr, pc)
            for pr in range(3)
            for pc in range(2)
            if -2 - (odd + pr) % 2 <= dr <= 3 - (odd + pr) % 2
            and -2 - pc <= dc <= 3 - pc
            and is_late(2 + pc + dc) == late
        ]
        if not used:
            continue
        cos_part = row_of(cos_ops, op, lanes)
        sin_part = row_of(sin_ops, op, lanes)
        for t in used:
            pr, pc = t
            source = parents[3 + pr + dr, 2 + pc + dc, :, lanes]
            source = source * present[24 + pr * 2 + pc, op]
            a, b = cos_part * source, sin_part * source
            first[t] = first[t] + a if t in first else a
            second[t] = second[t] + b if t in second else b
    return {t: first[t] + flip(second[t]) for t in first}


def far_early(parents, cos_ops, sin_ops, present, parent_in, core, odd):
    def one(n, carry):
        lanes = pl.ds(pl.multiple_of(n * 256, 256), 256)
        sums = far_sums(parents, cos_ops, sin_ops, present, lanes, core, odd, False)
        for (pr, pc), value in sums.items():
            parent_in[pr * 2 + pc, :, lanes] = value
        return carry

    lax.fori_loop(0, parent_in.shape[-1] // 256, one, 0)


def far_late(parents, cos_ops, sin_ops, present, parent_in, cosine, sine, child, core, odd):
    def one(n, carry):
        lanes = pl.ds(pl.multiple_of(n * 256, 256), 256)
        sums = far_sums(parents, cos_ops, sin_ops, present, lanes, core, odd, True)
        for pr in range(3):
            for pc in range(2):
                value = parent_in[pr * 2 + pc, :, lanes] + sums[(pr, pc)]
                value = value.astype(BF16).astype(F32)
                turned = flip(value)
                for kr in range(2):
                    both = [
                        row_of(cosine, 2 * kr + kc, lanes) * value - row_of(sine, 2 * kr + kc, lanes) * turned
                        for kc in range(2)
                    ]
                    box = (2 * pr + kr) * 4 + 2 * pc
                    child[box * 8 : box * 8 + 16, lanes] = jnp.concatenate(both, axis=0).astype(BF16)
        return carry

    lax.fori_loop(0, parent_in.shape[-1] // 256, one, 0)


def kernel(
    x_hbm, ops_hbm, interp_hbm, phase_hbm, fine_ops_hbm, fine_list_hbm, par_list_hbm, out,
    packed, own, oth, outr, opsg, x_raw, ops_raw, interp, phase, fine_ops, fine_list, par_list, on_vec, on,
    parents, window, near, parent_in, child, cosine, sine, cos_ops, sin_ops,
    ssem, rsem, fs, fr, lsem, ysem, zs, zr, es, er,
):
    np_, nd = lax.axis_size("patch"), lax.axis_size("dir")
    p, d = lax.axis_index("patch"), lax.axis_index("dir")
    core, z, y = lax.rem(d, 2), lax.rem(d // 2, ZN), d // (2 * ZN)
    odd = lax.rem(p, 2)
    up, down = lax.rem(p + 1, np_), lax.rem(p + np_ - 1, np_)
    other = d + 1 - 2 * core
    outer = lax.rem(d - 1 + 2 * core + nd, nd)
    far = lax.rem(d + 2 * ZN, nd)
    has_up, has_down = p < np_ - 1, p > 0
    has_outer = jnp.logical_and(d > 0, d < nd - 1)
    both_up, both_down = jnp.logical_and(has_outer, has_up), jnp.logical_and(has_outer, has_down)
    z_peer = [(p, y * 2 * ZN + lax.rem(z + k, ZN) * 2 + core) for k in range(ZN)]
    barrier = pltpu.get_barrier_semaphore()

    def greet(peer):
        pl.semaphore_signal(barrier, inc=1, device_id=peer, device_id_type=MESH)

    for peer in [(p, other), (p, far)] + z_peer[1:]:
        greet(peer)
    pl.when(has_up)(lambda: greet((up, d)))
    pl.when(has_down)(lambda: greet((down, d)))
    pl.when(has_outer)(lambda: greet((p, outer)))

    pairs = [
        (x_hbm, x_raw), (phase_hbm, phase), (interp_hbm, interp), (ops_hbm, ops_raw),
        (fine_list_hbm, fine_list), (par_list_hbm, par_list), (fine_ops_hbm, fine_ops),
    ]
    loads = [pltpu.make_async_copy(a, b, lsem.at[i]) for i, (a, b) in enumerate(pairs)]
    for load in loads:
        load.start()
    loads[1].wait()
    cosine[...] = jnp.cos(phase[...])
    sine[...] = jnp.sin(phase[...])
    loads[0].wait()
    for r in range(6):
        for c in range(0, 4, 2):
            parts = [x_raw[r, c + i // 2, i % 2].astype(F32) for i in range(4)]
            own[r + 2, c // 2] = jnp.concatenate(parts, axis=0).astype(BF16)
    loads[3].wait()
    opsg[core, z, y] = jnp.concatenate([ops_raw[:, 0, :], ops_raw[:, 1, :]], axis=1).astype(BF16)
    loads[2].wait()
    aggregate(own[2:8], interp, cosine, sine, packed, parents)

    one = lambda flag: flag.astype(jnp.int32)
    pl.semaphore_wait(barrier, 2 + ZN - 1 + one(has_up) + one(has_down) + one(has_outer))

    def send(src, dst, s, r, peer):
        return pltpu.make_async_remote_copy(
            src_ref=src, dst_ref=dst, send_sem=s, recv_sem=r, device_id=peer, device_id_type=MESH
        )

    def block(src, dst, peer):
        a, b = packed.at[pl.ds(src * 48, 48)], packed.at[pl.ds(dst * 48, 48)]
        return send(a, b, ssem.at[dst - 1], rsem.at[dst - 1], peer)

    def strip(slot, src, dst, peer):
        return send(src, dst, fs.at[slot - 1], fr.at[slot - 1], peer)

    low, mid, high = pl.ds(0, 2), pl.ds(2, 6), pl.ds(8, 2)
    first_rows, last_rows = pl.ds(2, 2), pl.ds(6, 2)
    routes = {
        1: (True, True, (p, other)),
        2: (has_outer, has_outer, (p, outer)),
        3: (has_up, has_down, (up, d)),
        4: (has_down, has_up, (down, d)),
        5: (has_down, has_down, (p, other)),
        6: (has_up, has_up, (p, other)),
        7: (both_up, both_down, (up, d)),
        8: (both_down, both_up, (down, d)),
    }
    source = {1: 0, 2: 0, 3: 0, 4: 0, 5: 3, 6: 4, 7: 2, 8: 2}
    blocks = {s: block(source[s], s, routes[s][2]) for s in routes}
    strips = {
        1: strip(1, own.at[mid, 1 - core], oth.at[mid], (p, other)),
        2: strip(2, own.at[mid, core], outr.at[mid], (p, outer)),
        3: strip(3, own.at[last_rows], own.at[low], (up, d)),
        4: strip(4, own.at[first_rows], own.at[high], (down, d)),
        5: strip(5, own.at[low, 1 - core], oth.at[low], (p, other)),
        6: strip(6, own.at[high, 1 - core], oth.at[high], (p, other)),
        7: strip(7, outr.at[last_rows], outr.at[low], (up, d)),
        8: strip(8, outr.at[first_rows], outr.at[high], (down, d)),
    }

    def when(flag, act):
        act() if flag is True else pl.when(flag)(act)

    def start(kind, slot):
        when(routes[slot][0], lambda: kind[slot].start())

    def arrive(kind, slot):
        when(routes[slot][1], lambda: kind[slot].wait_recv())

    own_ops, far_ops = opsg.at[core, z, y], opsg.at[core, z, 1 - y]
    to_far = send(own_ops, own_ops, ysem.at[0], ysem.at[1], (p, far))
    near_first = (1, 7, 2, 6, 3, 5, 4)

    def z_send(k, half):
        ref = opsg.at[core, z, y if half == 0 else 1 - y]
        return send(ref, ref, zs.at[half, k], zr.at[half, k], z_peer[k])

    def z_arrival(k, half):
        ref = opsg.at[core, lax.rem(z - k + ZN, ZN), y if half == 0 else 1 - y]
        return send(ref, ref, zs.at[half, k], zr.at[half, k], z_peer[k])

    def pass_on(k):
        ref = opsg.at[core, lax.rem(z - k + ZN, ZN)]
        return send(ref, ref, es.at[k], er.at[k], (p, other))

    to_far.start()
    for slot in (2, 3, 4, 1):
        start(strips, slot)
    for slot in (2, 3, 4):
        start(blocks, slot)
    for k in near_first:
        z_send(k, 0).start()
    start(blocks, 1)

    other_col, outer_col = 4 - 4 * core, 4 * core
    spots = {1: (3, other_col), 2: (3, outer_col), 3: (0, 2), 4: (6, 2), 5: (0, other_col), 6: (6, other_col),
             7: (0, outer_col), 8: (6, outer_col)}

    def settle(slot):
        row, col = spots[slot]
        arrive(blocks, slot)
        when(routes[slot][1], lambda: place(packed, slot, parents, row, col))
        if routes[slot][1] is not True:

            @pl.when(jnp.logical_not(routes[slot][1]))
            def _():
                for pr in range(3):
                    for pc in range(2):
                        parents[row + pr, col + pc] = jnp.zeros(parents.shape[2:], F32)

    def blank(ref, flag):
        @pl.when(jnp.logical_not(flag))
        def _():
            ref[...] = jnp.zeros(ref.shape, BF16)

    blank(own.at[low], has_down)
    blank(own.at[high], has_up)
    blank(oth.at[low], has_down)
    blank(oth.at[high], has_up)
    blank(outr.at[mid], has_outer)
    blank(outr.at[low], both_down)
    blank(outr.at[high], both_up)

    loads[4].wait()
    loads[5].wait()
    kind = lax.broadcasted_iota(jnp.int32, (32, 128), 1)
    for r in range(6):
        lists = fine_list[r]
        for c in range(4):
            mine = jnp.sum(jnp.where(kind == 4 * d + c, lists, 0), axis=1, keepdims=True)
            on_vec[r * 4 + c : r * 4 + c + 1, :] = jnp.sum(jnp.where(mine == kind, 1.0, 0.0), axis=0, keepdims=True)
    kind64 = lax.broadcasted_iota(jnp.int32, (32, 64), 1)
    for r in range(3):
        lists = par_list[r]
        for c in range(2):
            mine = jnp.sum(jnp.where(kind64 == 2 * d + c, lists, 0), axis=1, keepdims=True)
            row = 24 + r * 2 + c
            on_vec[row : row + 1, :] = jnp.sum(jnp.where(mine == kind, 1.0, 0.0), axis=0, keepdims=True)
    to_smem = pltpu.make_async_copy(on_vec, on, lsem.at[7])
    to_smem.start()

    arrive(strips, 3)
    start(strips, 5)
    arrive(strips, 4)
    start(strips, 6)
    to_far.wait()
    for k in near_first:
        z_send(k, 1).start()
    pass_on(0).start()
    arrive(strips, 1)
    for c in range(2):
        widen(lambda r, c=c: own[r, c], window, range(10), 2 + 2 * c)
    for slot in (5, 6):
        arrive(strips, slot)
    widen(lambda r: oth[r], window, range(10), 6 - 6 * core)
    settle(1)
    to_smem.wait()
    loads[6].wait()

    def near_part(late, begin, end):
        for which in range(2):
            pl.when(core == which)(
                lambda which=which: near_field(window, fine_ops, on, near, which, late, begin, end)
            )

    crossing = jnp.logical_or(d == 2 * ZN - 1, d == 2 * ZN)

    def relay(flag):
        @pl.when(jnp.logical_and(has_outer, flag))
        def _():
            strips[2].wait_recv()
            blocks[2].wait_recv()
            for slot in (7, 8):
                start(strips, slot)
                start(blocks, slot)

    relay(jnp.logical_not(crossing))
    near_part(False, 0, 4)
    relay(crossing)
    arrive(blocks, 3)
    start(blocks, 5)
    arrive(blocks, 4)
    start(blocks, 6)
    for k in near_first:
        z_arrival(k, 0).wait_recv()
        z_arrival(k, 1).wait_recv()
        pass_on(k).start()
    near_part(False, 4, 12)

    def place_only(slot):
        row, col = spots[slot]
        when(routes[slot][1], lambda: place(packed, slot, parents, row, col))
        if routes[slot][1] is not True:

            @pl.when(jnp.logical_not(routes[slot][1]))
            def _():
                for pr in range(3):
                    for pc in range(2):
                        parents[row + pr, col + pc] = jnp.zeros(parents.shape[2:], F32)

    for slot in (3, 4, 2):
        place_only(slot)
    for slot in (5, 6):
        settle(slot)
    for k in range(ZN):
        pass_on(k).wait_recv()

    def gather_ops(chunk, carry):
        lanes = pl.ds(pl.multiple_of(chunk * 128, 128), 128)
        even, uneven = (opsg[i, lax.rem(chunk, ZN), chunk // ZN].astype(F32) for i in range(2))
        left = lax.broadcasted_iota(jnp.int32, even.shape, 1) < 64
        cos_ops[:, lanes] = jnp.where(left, even, pltpu.roll(uneven, 64, 1))
        sin_ops[:, lanes] = jnp.where(left, pltpu.roll(even, 64, 1), uneven)
        return carry

    lax.fori_loop(0, 2 * ZN, gather_ops, 0)
    variants = [(a, b) for a in range(2) for b in range(2)]
    for a, b in variants:
        pl.when(jnp.logical_and(core == a, odd == b))(
            lambda a=a, b=b: far_early(parents, cos_ops, sin_ops, on, parent_in, a, b)
        )
    for slot in (7, 8):
        arrive(strips, slot)
    widen(lambda r: outr[r], window, range(10), 6 * core)
    near_part(True, 0, 12)
    for slot in (7, 8):
        settle(slot)
    for a, b in variants:
        pl.when(jnp.logical_and(core == a, odd == b))(
            lambda a=a, b=b: far_late(parents, cos_ops, sin_ops, on, parent_in, cosine, sine, child, a, b)
        )
    back = lax.dot_general(child[...], interp[...], (((1,), (1,)), ((), ())), preferred_element_type=F32)
    scale = interp.shape[0] / interp.shape[1]
    for r in range(6):
        for c in range(4):
            box = r * 4 + c
            total = near[box] + back[box * 8 : box * 8 + 8] * scale
            out[r, c, 0] = total[:4]
            out[r, c, 1] = total[4:]

    to_far_done = [z_send(k, half) for k in range(1, ZN) for half in range(2)] + [pass_on(k) for k in range(ZN)]
    for copy in to_far_done:
        copy.wait_send()
    for kind_of in (strips, blocks):
        for slot in routes:
            when(routes[slot][0], lambda kind_of=kind_of, slot=slot: kind_of[slot].wait_send())


def per_device(
    fine_out, interp, child_phase, fine_ops, parent_ops, fine_src, fine_op, parent_src, parent_op
):
    dp = interp.shape[1]
    kinds = fine_ops.shape[0]
    dma = pltpu.SemaphoreType.DMA
    hbm = pl.BlockSpec(memory_space=pl.ANY)
    vmem = pltpu.VMEM
    fine_list, par_list = (jnp.transpose(v, (0, 2, 1)) for v in (fine_op, parent_op))
    return pl.pallas_call(
        kernel,
        out_shape=jax.ShapeDtypeStruct(fine_out.shape, F32),
        in_specs=[hbm] * 7,
        out_specs=pl.BlockSpec(memory_space=pltpu.VMEM),
        scratch_shapes=[
            vmem((9 * 48, dp), BF16),
            vmem((10, 2, 16, 512), BF16),
            vmem((10, 16, 512), BF16),
            vmem((10, 16, 512), BF16),
            vmem((2, ZN, 2, kinds, 128), BF16),
            vmem(fine_out.shape, BF16),
            vmem(parent_ops.shape, F32),
            vmem(interp.shape, BF16),
            vmem((4, dp), F32),
            vmem(fine_ops.shape, F32),
            vmem(fine_list.shape, jnp.int32),
            vmem(par_list.shape, jnp.int32),
            vmem((32, 128), F32),
            pltpu.SMEM((32, 128), F32),
            vmem((9, 6, 8, dp), F32),
            vmem((10, 8, 8, 512), F32),
            vmem((24, 8, 512), F32),
            vmem((6, 8, dp), F32),
            vmem((192, dp), BF16),
            vmem((4, dp), F32),
            vmem((4, dp), F32),
            vmem((kinds, dp), F32),
            vmem((kinds, dp), F32),
            dma((8,)), dma((8,)), dma((8,)), dma((8,)), dma((8,)), dma((2,)),
            dma((2, ZN)), dma((2, ZN)), dma((ZN,)), dma((ZN,)),
        ],
        compiler_params=pltpu.CompilerParams(
            collective_id=0, has_side_effects=True, vmem_limit_bytes=56 * 1024 * 1024
        ),
        name="fmm",
    )(fine_out, parent_ops, interp, child_phase, fine_ops, fine_list, par_list)


def solution(mesh):
    in_specs = (
        P("patch", "dir", None, None, None),
        P(),
        P(),
        P(),
        P(None, None, "dir"),
        P("patch", None, None),
        P("patch", None, None),
        P("patch", None, None),
        P("patch", None, None),
    )
    out_specs = P("patch", "dir", None, None, None)
    return jax.shard_map(
        per_device, mesh=mesh, in_specs=in_specs, out_specs=out_specs, check_vma=False
    )
```

```python
import jax
import jax.numpy as jnp
from jax import lax
from jax.experimental import pallas as pl
from jax.experimental.pallas import tpu as pltpu
from jax.sharding import PartitionSpec as P

MESH = pl.DeviceIdType.MESH
ZN = 8
PIECE = 512
OWN, LEFT, RIGHT = (2, 3, 4, 5), (0, 1), (6, 7)
OFFSETS = [(a, b) for a in range(-3, 4) for b in range(-3, 4) if max(abs(a), abs(b)) > 1]
F32, BF16 = jnp.float32, jnp.bfloat16


def flip(v):
    turned = pltpu.roll(v, 4, 0)
    top = lax.broadcasted_iota(jnp.int32, v.shape, 0) < 4
    return jnp.where(top, -turned, turned)


def row_of(ref, r, lanes):
    return ref[pl.ds(r, 1), lanes]


def aggregate(own, interp, cosine, sine, packed, parents, q):
    rows = own[2:8].reshape(192, 512)
    for half in range(2):
        lanes = pl.ds(pl.multiple_of(q * PIECE + half * 256, 256), 256)
        spread = jnp.dot(rows, interp[:, lanes], preferred_element_type=F32)
        cos_at = [row_of(cosine, k, lanes) for k in range(4)]
        sin_at = [row_of(sine, k, lanes) for k in range(4)]
        for pr in range(3):
            pair = []
            for pc in range(2):
                first = second = None
                for k in range(4):
                    start = ((2 * pr + k // 2) * 4 + 2 * pc + k % 2) * 8
                    part = spread[start : start + 8]
                    a, b = cos_at[k] * part, sin_at[k] * part
                    first = a if first is None else first + a
                    second = b if second is None else second + b
                pair.append(first + flip(second))
            rounded = jnp.concatenate(pair, axis=0).astype(BF16)
            packed[q, pr * 16 : pr * 16 + 16, half * 256 : half * 256 + 256] = rounded
            wide = rounded.astype(F32)
            parents[3 + pr, 2, :, lanes] = wide[:8]
            parents[3 + pr, 3, :, lanes] = wide[8:]


def place(packed, slot, parents, row, col, q):
    lanes = pl.ds(pl.multiple_of(q * PIECE, PIECE), PIECE)
    for pr in range(3):
        wide = packed[q, slot * 48 + pr * 16 : slot * 48 + pr * 16 + 16, :].astype(F32)
        parents[row + pr, col, :, lanes] = wide[:8]
        parents[row + pr, col + 1, :, lanes] = wide[8:]


def widen(strip, window, rows, col_at):
    for r in rows:
        pair = strip(r).astype(F32)
        window[r, col_at] = pair[:8]
        window[r, col_at + 1] = pair[8:]


def near_field(window, ops, present, near, columns, start, stop):
    def one(step, carry):
        pair, lane = step // 4, lax.rem(step, 4)
        lanes = pl.ds(pl.multiple_of(lane * 128, 128), 128)
        first, second = {}, {}
        for op, (dr, dc) in enumerate(OFFSETS):
            used = [
                (kr, c)
                for kr in range(2)
                for c in range(4)
                if -2 - kr <= dr <= 3 - kr and -2 - c % 2 <= dc <= 3 - c % 2 and 2 + c + dc in columns
            ]
            if not used:
                continue
            cos_part = ops[op, pl.ds(0, 1), lanes]
            sin_part = ops[op, pl.ds(1, 1), lanes]
            for t in used:
                kr, c = t
                source = window[2 * pair + 2 + kr + dr, 2 + c + dc, :, lanes]
                source = source * present[(2 * pair + kr) * 4 + c, op]
                a, b = cos_part * source, sin_part * source
                first[t] = first[t] + a if t in first else a
                second[t] = second[t] + b if t in second else b
        for t in first:
            value = first[t] + flip(second[t])
            box = (2 * pair + t[0]) * 4 + t[1]
            near[box, :, lanes] = value if columns is OWN else near[box, :, lanes] + value
        return carry

    lax.fori_loop(start, stop, one, 0)


def far_sums(parents, cos_ops, sin_ops, present, lanes, core, odd, late):
    def is_late(col):
        return col < 2 if core == 0 else col >= 4

    first, second = {}, {}
    for op, (dr, dc) in enumerate(OFFSETS):
        used = [
            (pr, pc)
            for pr in range(3)
            for pc in range(2)
            if -2 - (odd + pr) % 2 <= dr <= 3 - (odd + pr) % 2
            and -2 - pc <= dc <= 3 - pc
            and is_late(2 + pc + dc) == late
        ]
        if not used:
            continue
        cos_part = row_of(cos_ops, op, lanes)
        sin_part = row_of(sin_ops, op, lanes)
        for t in used:
            pr, pc = t
            source = parents[3 + pr + dr, 2 + pc + dc, :, lanes]
            source = source * present[24 + pr * 2 + pc, op]
            a, b = cos_part * source, sin_part * source
            first[t] = first[t] + a if t in first else a
            second[t] = second[t] + b if t in second else b
    return {t: first[t] + flip(second[t]) for t in first}


def far_early(parents, cos_ops, sin_ops, present, parent_in, core, odd, q):
    def one(n, carry):
        lanes = pl.ds(pl.multiple_of(n * 256, 256), 256)
        sums = far_sums(parents, cos_ops, sin_ops, present, lanes, core, odd, False)
        for (pr, pc), value in sums.items():
            parent_in[pr * 2 + pc, :, lanes] = value
        return carry

    lax.fori_loop(q * (PIECE // 256), (q + 1) * (PIECE // 256), one, 0)


def far_late(parents, cos_ops, sin_ops, present, parent_in, cosine, sine, child, core, odd, q):
    def one(n, carry):
        lanes = pl.ds(pl.multiple_of(n * 256, 256), 256)
        sums = far_sums(parents, cos_ops, sin_ops, present, lanes, core, odd, True)
        for pr in range(3):
            for pc in range(2):
                value = parent_in[pr * 2 + pc, :, lanes] + sums[(pr, pc)]
                value = value.astype(BF16).astype(F32)
                turned = flip(value)
                for kr in range(2):
                    both = [
                        row_of(cosine, 2 * kr + kc, lanes) * value - row_of(sine, 2 * kr + kc, lanes) * turned
                        for kc in range(2)
                    ]
                    box = (2 * pr + kr) * 4 + 2 * pc
                    child[box * 8 : box * 8 + 16, lanes] = jnp.concatenate(both, axis=0).astype(BF16)
        return carry

    lax.fori_loop(q * (PIECE // 256), (q + 1) * (PIECE // 256), one, 0)


def kernel(
    x_hbm, ops_hbm, interp_hbm, phase_hbm, fine_ops_hbm, fine_list_hbm, par_list_hbm, out,
    packed, own, oth, outr, opsg, x_raw, ops_raw, interp, phase, fine_ops, fine_list, par_list, on_vec, on,
    parents, window, near, parent_in, child, cosine, sine, cos_ops, sin_ops,
    ssem, rsem, fs, fr, lsem, isem, ysem, zs, zr, es, er,
):
    np_, nd = lax.axis_size("patch"), lax.axis_size("dir")
    p, d = lax.axis_index("patch"), lax.axis_index("dir")
    core, z, y = lax.rem(d, 2), lax.rem(d // 2, ZN), d // (2 * ZN)
    odd = lax.rem(p, 2)
    up, down = lax.rem(p + 1, np_), lax.rem(p + np_ - 1, np_)
    other = d + 1 - 2 * core
    outer = lax.rem(d - 1 + 2 * core + nd, nd)
    far = lax.rem(d + 2 * ZN, nd)
    has_up, has_down = p < np_ - 1, p > 0
    has_outer = jnp.logical_and(d > 0, d < nd - 1)
    both_up, both_down = jnp.logical_and(has_outer, has_up), jnp.logical_and(has_outer, has_down)
    z_peer = [(p, y * 2 * ZN + lax.rem(z + k, ZN) * 2 + core) for k in range(ZN)]
    barrier = pltpu.get_barrier_semaphore()

    def greet(peer):
        pl.semaphore_signal(barrier, inc=1, device_id=peer, device_id_type=MESH)

    for peer in [(p, other), (p, far)] + z_peer[1:]:
        greet(peer)
    pl.when(has_up)(lambda: greet((up, d)))
    pl.when(has_down)(lambda: greet((down, d)))
    pl.when(has_outer)(lambda: greet((p, outer)))

    pieces = interp.shape[1] // PIECE
    pairs = [
        (x_hbm, x_raw), (phase_hbm, phase), (ops_hbm, ops_raw),
        (fine_list_hbm, fine_list), (par_list_hbm, par_list), (fine_ops_hbm, fine_ops),
    ]
    loads = [pltpu.make_async_copy(a, b, lsem.at[i]) for i, (a, b) in enumerate(pairs)]

    def interp_load(q):
        lanes = pl.ds(pl.multiple_of(q * PIECE, PIECE), PIECE)
        return pltpu.make_async_copy(interp_hbm.at[:, lanes], interp.at[:, lanes], isem.at[q])

    for load in loads[:2]:
        load.start()
    for q in range(pieces):
        interp_load(q).start()
    for load in loads[2:]:
        load.start()
    loads[1].wait()
    cosine[...] = jnp.cos(phase[...])
    sine[...] = jnp.sin(phase[...])
    loads[0].wait()
    for r in range(6):
        for c in range(0, 4, 2):
            parts = [x_raw[r, c + i // 2, i % 2].astype(F32) for i in range(4)]
            own[r + 2, c // 2] = jnp.concatenate(parts, axis=0).astype(BF16)
    loads[2].wait()
    opsg[core, z, y] = jnp.concatenate([ops_raw[:, 0, :], ops_raw[:, 1, :]], axis=1).astype(opsg.dtype)

    one = lambda flag: flag.astype(jnp.int32)
    pl.semaphore_wait(barrier, 2 + ZN - 1 + one(has_up) + one(has_down) + one(has_outer))

    def send(src, dst, s, r, peer):
        return pltpu.make_async_remote_copy(
            src_ref=src, dst_ref=dst, send_sem=s, recv_sem=r, device_id=peer, device_id_type=MESH
        )

    def strip(slot, src, dst, peer):
        return send(src, dst, fs.at[slot - 1], fr.at[slot - 1], peer)

    low, mid, high = pl.ds(0, 2), pl.ds(2, 6), pl.ds(8, 2)
    first_rows, last_rows = pl.ds(2, 2), pl.ds(6, 2)
    routes = {
        1: (True, True, (p, other)),
        2: (has_outer, has_outer, (p, outer)),
        3: (has_up, has_down, (up, d)),
        4: (has_down, has_up, (down, d)),
        5: (has_down, has_down, (p, other)),
        6: (has_up, has_up, (p, other)),
        7: (both_up, both_down, (up, d)),
        8: (both_down, both_up, (down, d)),
    }
    source = {1: 0, 2: 0, 3: 0, 4: 0, 5: 3, 6: 4, 7: 2, 8: 2}

    even = odd == 0
    not_even = odd == 1
    short_send = {3: not_even, 4: even, 5: even, 6: not_even, 7: not_even, 8: even}
    short_recv = {3: even, 4: not_even, 5: even, 6: not_even, 7: even, 8: not_even}

    def block(slot, q, short=False, src=None, peer=None):
        first, count = (16 if slot % 2 else 0, 32) if short else (0, 48)
        src = source[slot] if src is None else src
        a, b = (packed.at[q, pl.ds(i * 48 + first, count)] for i in (src, slot))
        return send(a, b, ssem.at[q, slot - 1], rsem.at[q, slot - 1], routes[slot][2] if peer is None else peer)

    def each_size(slot, flag, short, act):
        if slot < 3:
            when(flag, lambda: act(False))
        else:
            pl.when(jnp.logical_and(flag, short[slot]))(lambda: act(True))
            pl.when(jnp.logical_and(flag, jnp.logical_not(short[slot])))(lambda: act(False))

    strips = {
        1: strip(1, own.at[mid, 1 - core], oth.at[mid], (p, other)),
        2: strip(2, own.at[mid, core], outr.at[mid], (p, outer)),
        3: strip(3, own.at[last_rows], own.at[low], (up, d)),
        4: strip(4, own.at[first_rows], own.at[high], (down, d)),
        5: strip(5, own.at[low, 1 - core], oth.at[low], (p, other)),
        6: strip(6, own.at[high, 1 - core], oth.at[high], (p, other)),
        7: strip(7, outr.at[last_rows], outr.at[low], (up, d)),
        8: strip(8, outr.at[first_rows], outr.at[high], (down, d)),
    }

    def when(flag, act):
        act() if flag is True else pl.when(flag)(act)

    def start(slot):
        when(routes[slot][0], lambda: strips[slot].start())

    def arrive(slot):
        when(routes[slot][1], lambda: strips[slot].wait_recv())

    def start_block(slot, q):
        each_size(slot, sends[slot], short_send, lambda short: block(slot, q, short).start())

    def arrive_block(slot, q):
        each_size(slot, routes[slot][1], short_recv, lambda short: block(slot, q, short).wait_recv())

    def sent_block(slot, q):
        each_size(slot, sends[slot], short_send, lambda short: block(slot, q, short).wait_send())

    def across(slot, q):
        return block(slot, q, True, slot - 4, (p, outer))

    crossing = jnp.logical_or(d == 2 * ZN - 1, d == 2 * ZN)
    direct = jnp.logical_and(has_outer, jnp.logical_not(crossing))
    run = 4
    edge_low = jnp.logical_and(lax.rem(p, run) == 0, has_down)
    edge_high = jnp.logical_and(lax.rem(p, run) == run - 1, has_up)
    hand_on = {7: jnp.logical_and(direct, edge_low), 8: jnp.logical_and(direct, edge_high)}
    sends = {s: routes[s][0] for s in routes}
    sends[7] = jnp.logical_and(both_up, jnp.logical_not(hand_on[8]))
    sends[8] = jnp.logical_and(both_down, jnp.logical_not(hand_on[7]))

    own_ops = opsg.at[core, z, y]
    to_far = send(own_ops, own_ops, ysem.at[0], ysem.at[1], (p, far))
    near_first = (1, 7, 2, 6, 3, 5, 4)

    def z_send(k, half):
        ref = opsg.at[core, z, y if half == 0 else 1 - y]
        return send(ref, ref, zs.at[half, k], zr.at[half, k], z_peer[k])

    def z_arrival(k, half):
        ref = opsg.at[core, lax.rem(z - k + ZN, ZN), y if half == 0 else 1 - y]
        return send(ref, ref, zs.at[half, k], zr.at[half, k], z_peer[k])

    def pass_on(k, half):
        ref = opsg.at[core, lax.rem(z - k + ZN, ZN), y if half == 0 else 1 - y]
        return send(ref, ref, es.at[half, k], er.at[half, k], (p, other))

    for slot in (2, 3, 4, 1):
        start(slot)
    to_far.start()
    for k in near_first:
        z_send(k, 0).start()

    def following(q, carry):
        interp_load(q).wait()
        aggregate(own, interp, cosine, sine, packed, parents, q)
        for slot in (2, 3, 4, 1):
            start_block(slot, q)
        return carry

    lax.fori_loop(0, pieces, following, 0)

    other_col, outer_col = 4 - 4 * core, 4 * core
    spots = {1: (3, other_col), 2: (3, outer_col), 3: (0, 2), 4: (6, 2), 5: (0, other_col), 6: (6, other_col),
             7: (0, outer_col), 8: (6, outer_col)}

    def settle(slot, q):
        row, col = spots[slot]
        when(routes[slot][1], lambda: place(packed, slot, parents, row, col, q))

    for slot in range(2, 9):

        @pl.when(jnp.logical_not(routes[slot][1]))
        def _(slot=slot):
            row, col = spots[slot]
            for pr in range(3):
                for pc in range(2):
                    parents[row + pr, col + pc] = jnp.zeros(parents.shape[2:], F32)

    def blank(ref, flag):
        @pl.when(jnp.logical_not(flag))
        def _():
            ref[...] = jnp.zeros(ref.shape, BF16)

    blank(own.at[low], has_down)
    blank(own.at[high], has_up)
    blank(oth.at[low], has_down)
    blank(oth.at[high], has_up)
    blank(outr.at[mid], has_outer)
    blank(outr.at[low], both_down)
    blank(outr.at[high], both_up)

    loads[3].wait()
    loads[4].wait()
    kind = lax.broadcasted_iota(jnp.int32, (32, 128), 1)
    for r in range(6):
        lists = fine_list[r]
        for c in range(4):
            mine = jnp.sum(jnp.where(kind == 4 * d + c, lists, 0), axis=1, keepdims=True)
            on_vec[r * 4 + c : r * 4 + c + 1, :] = jnp.sum(jnp.where(mine == kind, 1.0, 0.0), axis=0, keepdims=True)
    kind64 = lax.broadcasted_iota(jnp.int32, (32, 64), 1)
    for r in range(3):
        lists = par_list[r]
        for c in range(2):
            mine = jnp.sum(jnp.where(kind64 == 2 * d + c, lists, 0), axis=1, keepdims=True)
            row = 24 + r * 2 + c
            on_vec[row : row + 1, :] = jnp.sum(jnp.where(mine == kind, 1.0, 0.0), axis=0, keepdims=True)
    to_smem = pltpu.make_async_copy(on_vec, on, lsem.at[6])
    to_smem.start()

    def relay(q):
        block(2, q).wait_recv()
        for slot in (7, 8):
            start_block(slot, q)

    def relay_strips():
        strips[2].wait_recv()
        for slot in (7, 8):
            start(slot)

    def forward(q):
        for slot in (3, 4):
            arrive_block(slot, q)
            start_block(slot + 2, q)
            pl.when(hand_on[slot + 4])(lambda slot=slot: across(slot + 4, q).start())
        pl.when(direct)(lambda: relay(q))

    def near_side(columns_of):
        for which in range(2):
            pl.when(core == which)(
                lambda which=which: near_field(window, fine_ops, on, near, columns_of[which], 0, 12)
            )

    def relay_crossing(*qs):
        @pl.when(crossing)
        def _():
            for q in qs:
                relay(q)

    def collect(half):
        for k in near_first:
            z_arrival(k, half).wait_recv()
            pass_on(k, half).start()

    for slot in (3, 4):
        arrive(slot)
        start(slot + 2)
    for c in range(2):
        widen(lambda r, c=c: own[r, c], window, range(10), 2 + 2 * c)
    to_smem.wait()
    loads[5].wait()
    near_field(window, fine_ops, on, near, OWN, 0, 4)
    to_far.wait()
    for k in near_first:
        z_send(k, 1).start()
    for half in range(2):
        pass_on(0, half).start()
    forward(0)
    near_field(window, fine_ops, on, near, OWN, 4, 8)
    forward(1)
    pl.when(direct)(relay_strips)
    near_field(window, fine_ops, on, near, OWN, 8, 12)
    collect(0)
    forward(2)
    for slot in (1, 5, 6):
        arrive(slot)
    widen(lambda r: oth[r], window, range(10), 6 - 6 * core)
    near_side((RIGHT, LEFT))
    forward(3)

    def gather_ops(chunk, carry):
        lanes = pl.ds(pl.multiple_of(chunk * 128, 128), 128)
        even, uneven = (opsg[i, lax.rem(chunk, ZN), chunk // ZN].astype(F32) for i in range(2))
        left = lax.broadcasted_iota(jnp.int32, even.shape, 1) < 64
        cos_ops[:, lanes] = jnp.where(left, even, pltpu.roll(uneven, 64, 1))
        sin_ops[:, lanes] = jnp.where(left, pltpu.roll(even, 64, 1), uneven)
        return carry

    variants = [(a, b) for a in range(2) for b in range(2)]

    half_pieces = pieces // 2

    def early(i, carry):
        q = lax.rem(half_pieces * y + i, pieces)
        for slot in (1, 5, 6):
            arrive_block(slot, q)
        for slot in (1, 3, 4, 5, 6):
            settle(slot, q)
        lax.fori_loop(q * (PIECE // 128), (q + 1) * (PIECE // 128), gather_ops, 0)
        for a, b in variants:
            pl.when(jnp.logical_and(core == a, odd == b))(
                lambda a=a, b=b: far_early(parents, cos_ops, sin_ops, on, parent_in, a, b, q)
            )
        return carry

    for k in range(ZN):
        pass_on(k, 0).wait_recv()
    lax.fori_loop(0, half_pieces, early, 0)
    collect(1)
    pl.when(crossing)(relay_strips)
    relay_crossing(*range(pieces))
    for k in range(ZN):
        pass_on(k, 1).wait_recv()
    lax.fori_loop(half_pieces, pieces, early, 0)
    for slot in (7, 8):
        arrive(slot)
    widen(lambda r: outr[r], window, range(10), 6 * core)
    near_side((LEFT, RIGHT))
    scale = interp.shape[0] / interp.shape[1]

    def last(q, carry):
        settle(2, q)
        for slot in (7, 8):
            arrive_block(slot, q)
            settle(slot, q)
        for a, b in variants:
            pl.when(jnp.logical_and(core == a, odd == b))(
                lambda a=a, b=b: far_late(parents, cos_ops, sin_ops, on, parent_in, cosine, sine, child, a, b, q)
            )
        lanes = pl.ds(pl.multiple_of(q * PIECE, PIECE), PIECE)
        back = lax.dot_general(
            child[:, lanes], interp[:, lanes], (((1,), (1,)), ((), ())), preferred_element_type=F32
        )
        near[...] += (back * scale).reshape(near.shape)
        return carry

    lax.fori_loop(0, pieces, last, 0)
    for r in range(6):
        for c in range(4):
            total = near[r * 4 + c]
            out[r, c, 0] = total[:4]
            out[r, c, 1] = total[4:]

    for copy in [z_send(k, half) for k in range(1, ZN) for half in range(2)] + [
        pass_on(k, half) for k in range(ZN) for half in range(2)
    ]:
        copy.wait_send()
    for slot in routes:
        when(routes[slot][0], lambda slot=slot: strips[slot].wait_send())

    def drain(q, carry):
        for slot in routes:
            sent_block(slot, q)
        for slot in (7, 8):
            pl.when(hand_on[slot])(lambda slot=slot: across(slot, q).wait_send())
        return carry

    lax.fori_loop(0, pieces, drain, 0)


def per_device(
    fine_out, interp, child_phase, fine_ops, parent_ops, fine_src, fine_op, parent_src, parent_op
):
    dp = interp.shape[1]
    kinds = fine_ops.shape[0]
    dma = pltpu.SemaphoreType.DMA
    hbm = pl.BlockSpec(memory_space=pl.ANY)
    vmem = pltpu.VMEM
    fine_list, par_list = (jnp.transpose(v, (0, 2, 1)) for v in (fine_op, parent_op))
    return pl.pallas_call(
        kernel,
        out_shape=jax.ShapeDtypeStruct(fine_out.shape, F32),
        in_specs=[hbm] * 7,
        out_specs=pl.BlockSpec(memory_space=pltpu.VMEM),
        scratch_shapes=[
            vmem((dp // PIECE, 9 * 48, PIECE), BF16),
            vmem((10, 2, 16, 512), BF16),
            vmem((10, 16, 512), BF16),
            vmem((10, 16, 512), BF16),
            vmem((2, ZN, 2, kinds, 128), BF16),
            vmem(fine_out.shape, BF16),
            vmem(parent_ops.shape, F32),
            vmem(interp.shape, BF16),
            vmem((4, dp), F32),
            vmem(fine_ops.shape, F32),
            vmem(fine_list.shape, jnp.int32),
            vmem(par_list.shape, jnp.int32),
            vmem((32, 128), F32),
            pltpu.SMEM((32, 128), F32),
            vmem((9, 6, 8, dp), F32),
            vmem((10, 8, 8, 512), F32),
            vmem((24, 8, 512), F32),
            vmem((6, 8, dp), F32),
            vmem((192, dp), BF16),
            vmem((4, dp), F32),
            vmem((4, dp), F32),
            vmem((kinds, dp), F32),
            vmem((kinds, dp), F32),
            dma((dp // PIECE, 8)), dma((dp // PIECE, 8)), dma((8,)), dma((8,)), dma((8,)), dma((dp // PIECE,)), dma((2,)),
            dma((2, ZN)), dma((2, ZN)), dma((2, ZN)), dma((2, ZN)),
        ],
        compiler_params=pltpu.CompilerParams(
            collective_id=0, has_side_effects=True, vmem_limit_bytes=56 * 1024 * 1024
        ),
        name="fmm",
    )(fine_out, parent_ops, interp, child_phase, fine_ops, fine_list, par_list)


def solution(mesh):
    in_specs = (
        P("patch", "dir", None, None, None),
        P(),
        P(),
        P(),
        P(None, None, "dir"),
        P("patch", None, None),
        P("patch", None, None),
        P("patch", None, None),
        P("patch", None, None),
    )
    out_specs = P("patch", "dir", None, None, None)
    return jax.shard_map(
        per_device, mesh=mesh, in_specs=in_specs, out_specs=out_specs, check_vma=False
    )
```

```python
import jax
import jax.numpy as jnp
from jax import lax
from jax.experimental import pallas as pl
from jax.experimental.pallas import tpu as pltpu
from jax.sharding import PartitionSpec as P

MESH = pl.DeviceIdType.MESH
ZN = 8
PIECE = 512
OWN, LEFT, RIGHT = (2, 3, 4, 5), (0, 1), (6, 7)
OFFSETS = [(a, b) for a in range(-3, 4) for b in range(-3, 4) if max(abs(a), abs(b)) > 1]
F32, BF16 = jnp.float32, jnp.bfloat16


def flip(v):
    turned = pltpu.roll(v, 4, 0)
    top = lax.broadcasted_iota(jnp.int32, v.shape, 0) < 4
    return jnp.where(top, -turned, turned)


def row_of(ref, r, lanes):
    return ref[pl.ds(r, 1), lanes]


def aggregate(own, interp, cosine, sine, packed, parents, q):
    rows = own[2:8].reshape(192, 512)
    for half in range(2):
        lanes = pl.ds(pl.multiple_of(q * PIECE + half * 256, 256), 256)
        spread = jnp.dot(rows, interp[:, lanes], preferred_element_type=F32)
        cos_at = [row_of(cosine, k, lanes) for k in range(4)]
        sin_at = [row_of(sine, k, lanes) for k in range(4)]
        for pr in range(3):
            pair = []
            for pc in range(2):
                first = second = None
                for k in range(4):
                    start = ((2 * pr + k // 2) * 4 + 2 * pc + k % 2) * 8
                    part = spread[start : start + 8]
                    a, b = cos_at[k] * part, sin_at[k] * part
                    first = a if first is None else first + a
                    second = b if second is None else second + b
                pair.append(first + flip(second))
            rounded = jnp.concatenate(pair, axis=0).astype(BF16)
            packed[q, pr * 16 : pr * 16 + 16, half * 256 : half * 256 + 256] = rounded
            wide = rounded.astype(F32)
            parents[3 + pr, 2, :, lanes] = wide[:8]
            parents[3 + pr, 3, :, lanes] = wide[8:]


def place(packed, slot, parents, row, col, q):
    lanes = pl.ds(pl.multiple_of(q * PIECE, PIECE), PIECE)
    for pr in range(3):
        wide = packed[q, slot * 48 + pr * 16 : slot * 48 + pr * 16 + 16, :].astype(F32)
        parents[row + pr, col, :, lanes] = wide[:8]
        parents[row + pr, col + 1, :, lanes] = wide[8:]


def widen(strip, window, rows, col_at):
    for r in rows:
        pair = strip(r).astype(F32)
        window[r, col_at] = pair[:8]
        window[r, col_at + 1] = pair[8:]


def near_field(window, ops, present, near, columns, start, stop):
    def one(step, carry):
        pair, lane = step // 2, lax.rem(step, 2)
        lanes = pl.ds(pl.multiple_of(lane * 256, 256), 256)
        first, second = {}, {}
        for op, (dr, dc) in enumerate(OFFSETS):
            used = [
                (kr, c)
                for kr in range(2)
                for c in range(4)
                if -2 - kr <= dr <= 3 - kr and -2 - c % 2 <= dc <= 3 - c % 2 and 2 + c + dc in columns
            ]
            if not used:
                continue
            cos_part = ops[op, pl.ds(0, 1), lanes]
            sin_part = ops[op, pl.ds(1, 1), lanes]
            for t in used:
                kr, c = t
                source = window[2 * pair + 2 + kr + dr, 2 + c + dc, :, lanes]
                source = source * present[(2 * pair + kr) * 4 + c, op]
                a, b = cos_part * source, sin_part * source
                first[t] = first[t] + a if t in first else a
                second[t] = second[t] + b if t in second else b
        for t in first:
            value = first[t] + flip(second[t])
            box = (2 * pair + t[0]) * 4 + t[1]
            near[box, :, lanes] = value if columns is OWN else near[box, :, lanes] + value
        return carry

    lax.fori_loop(start, stop, one, 0)


def far_sums(parents, cos_ops, sin_ops, present, lanes, core, odd, late):
    def is_late(col):
        return col < 2 if core == 0 else col >= 4

    first, second = {}, {}
    for op, (dr, dc) in enumerate(OFFSETS):
        used = [
            (pr, pc)
            for pr in range(3)
            for pc in range(2)
            if -2 - (odd + pr) % 2 <= dr <= 3 - (odd + pr) % 2
            and -2 - pc <= dc <= 3 - pc
            and is_late(2 + pc + dc) == late
        ]
        if not used:
            continue
        cos_part = row_of(cos_ops, op, lanes)
        sin_part = row_of(sin_ops, op, lanes)
        for t in used:
            pr, pc = t
            source = parents[3 + pr + dr, 2 + pc + dc, :, lanes]
            source = source * present[24 + pr * 2 + pc, op]
            a, b = cos_part * source, sin_part * source
            first[t] = first[t] + a if t in first else a
            second[t] = second[t] + b if t in second else b
    return {t: first[t] + flip(second[t]) for t in first}


def far_early(parents, cos_ops, sin_ops, present, parent_in, core, odd, q):
    def one(n, carry):
        lanes = pl.ds(pl.multiple_of(n * 256, 256), 256)
        sums = far_sums(parents, cos_ops, sin_ops, present, lanes, core, odd, False)
        for (pr, pc), value in sums.items():
            parent_in[pr * 2 + pc, :, lanes] = value
        return carry

    lax.fori_loop(q * (PIECE // 256), (q + 1) * (PIECE // 256), one, 0)


def far_late(parents, cos_ops, sin_ops, present, parent_in, cosine, sine, child, core, odd, q):
    def one(n, carry):
        lanes = pl.ds(pl.multiple_of(n * 256, 256), 256)
        sums = far_sums(parents, cos_ops, sin_ops, present, lanes, core, odd, True)
        for pr in range(3):
            for pc in range(2):
                value = parent_in[pr * 2 + pc, :, lanes] + sums[(pr, pc)]
                value = value.astype(BF16).astype(F32)
                turned = flip(value)
                for kr in range(2):
                    both = [
                        row_of(cosine, 2 * kr + kc, lanes) * value - row_of(sine, 2 * kr + kc, lanes) * turned
                        for kc in range(2)
                    ]
                    box = (2 * pr + kr) * 4 + 2 * pc
                    child[box * 8 : box * 8 + 16, lanes] = jnp.concatenate(both, axis=0).astype(BF16)
        return carry

    lax.fori_loop(q * (PIECE // 256), (q + 1) * (PIECE // 256), one, 0)


def kernel(
    x_hbm, ops_hbm, interp_hbm, phase_hbm, fine_ops_hbm, fine_list_hbm, par_list_hbm, out,
    packed, own, oth, outr, opsg, x_raw, ops_raw, interp, phase, fine_ops, fine_list, par_list, on_vec, on,
    parents, window, near, parent_in, child, cosine, sine, cos_ops, sin_ops,
    ssem, rsem, fs, fr, lsem, isem, ysem, zs, zr, es, er,
):
    np_, nd = lax.axis_size("patch"), lax.axis_size("dir")
    p, d = lax.axis_index("patch"), lax.axis_index("dir")
    core, z, y = lax.rem(d, 2), lax.rem(d // 2, ZN), d // (2 * ZN)
    odd = lax.rem(p, 2)
    up, down = lax.rem(p + 1, np_), lax.rem(p + np_ - 1, np_)
    other = d + 1 - 2 * core
    outer = lax.rem(d - 1 + 2 * core + nd, nd)
    far = lax.rem(d + 2 * ZN, nd)
    has_up, has_down = p < np_ - 1, p > 0
    has_outer = jnp.logical_and(d > 0, d < nd - 1)
    both_up, both_down = jnp.logical_and(has_outer, has_up), jnp.logical_and(has_outer, has_down)
    z_peer = [(p, y * 2 * ZN + lax.rem(z + k, ZN) * 2 + core) for k in range(ZN)]
    barrier = pltpu.get_barrier_semaphore()

    def greet(peer):
        pl.semaphore_signal(barrier, inc=1, device_id=peer, device_id_type=MESH)

    for peer in [(p, other), (p, far)] + z_peer[1:]:
        greet(peer)
    pl.when(has_up)(lambda: greet((up, d)))
    pl.when(has_down)(lambda: greet((down, d)))
    pl.when(has_outer)(lambda: greet((p, outer)))

    pieces = interp.shape[1] // PIECE
    pairs = [
        (x_hbm, x_raw), (phase_hbm, phase), (ops_hbm, ops_raw),
        (fine_list_hbm, fine_list), (par_list_hbm, par_list), (fine_ops_hbm, fine_ops),
    ]
    loads = [pltpu.make_async_copy(a, b, lsem.at[i]) for i, (a, b) in enumerate(pairs)]

    def interp_load(q):
        lanes = pl.ds(pl.multiple_of(q * PIECE, PIECE), PIECE)
        return pltpu.make_async_copy(interp_hbm.at[:, lanes], interp.at[:, lanes], isem.at[q])

    for load in loads[:2]:
        load.start()
    half_pieces = pieces // 2

    def turn(i, half=y):
        return lax.rem(half_pieces * half + i, pieces)

    for i in range(pieces):
        interp_load(turn(i)).start()
    for load in loads[2:]:
        load.start()
    loads[1].wait()
    cosine[...] = jnp.cos(phase[...])
    sine[...] = jnp.sin(phase[...])
    loads[0].wait()
    for r in range(6):
        for c in range(0, 4, 2):
            parts = [x_raw[r, c + i // 2, i % 2].astype(F32) for i in range(4)]
            own[r + 2, c // 2] = jnp.concatenate(parts, axis=0).astype(BF16)
    loads[2].wait()
    opsg[core, z, y] = jnp.concatenate([ops_raw[:, 0, :], ops_raw[:, 1, :]], axis=1).astype(opsg.dtype)

    one = lambda flag: flag.astype(jnp.int32)
    pl.semaphore_wait(barrier, 2 + ZN - 1 + one(has_up) + one(has_down) + one(has_outer))

    def send(src, dst, s, r, peer):
        return pltpu.make_async_remote_copy(
            src_ref=src, dst_ref=dst, send_sem=s, recv_sem=r, device_id=peer, device_id_type=MESH
        )

    def strip(slot, src, dst, peer):
        return send(src, dst, fs.at[slot - 1], fr.at[slot - 1], peer)

    low, mid, high = pl.ds(0, 2), pl.ds(2, 6), pl.ds(8, 2)
    first_rows, last_rows = pl.ds(2, 2), pl.ds(6, 2)
    routes = {
        1: (True, True, (p, other)),
        2: (has_outer, has_outer, (p, outer)),
        3: (has_up, has_down, (up, d)),
        4: (has_down, has_up, (down, d)),
        5: (has_down, has_down, (p, other)),
        6: (has_up, has_up, (p, other)),
        7: (both_up, both_down, (up, d)),
        8: (both_down, both_up, (down, d)),
    }
    source = {1: 0, 2: 0, 3: 0, 4: 0, 5: 3, 6: 4, 7: 2, 8: 2}

    even = odd == 0
    not_even = odd == 1
    short_send = {3: not_even, 4: even, 5: even, 6: not_even, 7: not_even, 8: even}
    short_recv = {3: even, 4: not_even, 5: even, 6: not_even, 7: even, 8: not_even}

    def block(slot, q, short=False, src=None, peer=None):
        first, count = (16 if slot % 2 else 0, 32) if short else (0, 48)
        src = source[slot] if src is None else src
        a, b = (packed.at[q, pl.ds(i * 48 + first, count)] for i in (src, slot))
        return send(a, b, ssem.at[q, slot - 1], rsem.at[q, slot - 1], routes[slot][2] if peer is None else peer)

    def each_size(slot, flag, short, act):
        if slot < 3:
            when(flag, lambda: act(False))
        else:
            pl.when(jnp.logical_and(flag, short[slot]))(lambda: act(True))
            pl.when(jnp.logical_and(flag, jnp.logical_not(short[slot])))(lambda: act(False))

    strips = {
        1: strip(1, own.at[mid, 1 - core], oth.at[mid], (p, other)),
        2: strip(2, own.at[mid, core], outr.at[mid], (p, outer)),
        3: strip(3, own.at[last_rows], own.at[low], (up, d)),
        4: strip(4, own.at[first_rows], own.at[high], (down, d)),
        5: strip(5, own.at[low, 1 - core], oth.at[low], (p, other)),
        6: strip(6, own.at[high, 1 - core], oth.at[high], (p, other)),
        7: strip(7, outr.at[last_rows], outr.at[low], (up, d)),
        8: strip(8, outr.at[first_rows], outr.at[high], (down, d)),
    }

    def when(flag, act):
        act() if flag is True else pl.when(flag)(act)

    def start(slot):
        when(routes[slot][0], lambda: strips[slot].start())

    def arrive(slot):
        when(routes[slot][1], lambda: strips[slot].wait_recv())

    def start_block(slot, q):
        each_size(slot, sends[slot], short_send, lambda short: block(slot, q, short).start())

    def arrive_block(slot, q):
        each_size(slot, routes[slot][1], short_recv, lambda short: block(slot, q, short).wait_recv())

    def sent_block(slot, q):
        each_size(slot, sends[slot], short_send, lambda short: block(slot, q, short).wait_send())

    def across(slot, q):
        return block(slot, q, True, slot - 4, (p, outer))

    crossing = jnp.logical_or(d == 2 * ZN - 1, d == 2 * ZN)
    direct = jnp.logical_and(has_outer, jnp.logical_not(crossing))
    run = 4
    edge_low = jnp.logical_and(lax.rem(p, run) == 0, has_down)
    edge_high = jnp.logical_and(lax.rem(p, run) == run - 1, has_up)
    hand_on = {7: jnp.logical_and(direct, edge_low), 8: jnp.logical_and(direct, edge_high)}
    sends = {s: routes[s][0] for s in routes}
    sends[7] = jnp.logical_and(both_up, jnp.logical_not(hand_on[8]))
    sends[8] = jnp.logical_and(both_down, jnp.logical_not(hand_on[7]))

    own_ops = opsg.at[core, z, y]
    to_far = send(own_ops, own_ops, ysem.at[0], ysem.at[1], (p, far))
    near_first = (1, 7, 2, 6, 3, 5, 4)

    def z_send(k, half):
        ref = opsg.at[core, z, y if half == 0 else 1 - y]
        return send(ref, ref, zs.at[half, k], zr.at[half, k], z_peer[k])

    def z_arrival(k, half):
        ref = opsg.at[core, lax.rem(z - k + ZN, ZN), y if half == 0 else 1 - y]
        return send(ref, ref, zs.at[half, k], zr.at[half, k], z_peer[k])

    def pass_on(k, half):
        ref = opsg.at[core, lax.rem(z - k + ZN, ZN), y if half == 0 else 1 - y]
        return send(ref, ref, es.at[half, k], er.at[half, k], (p, other))

    patient = d == 2 * ZN

    to_far.start()
    pl.when(jnp.logical_not(patient))(lambda: start(2))
    for slot in (3, 4, 1):
        start(slot)
    for k in near_first:
        z_send(k, 0).start()

    def following(i, carry):
        q = turn(i)
        interp_load(q).wait()
        aggregate(own, interp, cosine, sine, packed, parents, q)
        pl.when(jnp.logical_not(patient))(lambda: start_block(2, q))
        for slot in (3, 4, 1):
            start_block(slot, q)
        return carry

    lax.fori_loop(0, pieces, following, 0)

    other_col, outer_col = 4 - 4 * core, 4 * core
    spots = {1: (3, other_col), 2: (3, outer_col), 3: (0, 2), 4: (6, 2), 5: (0, other_col), 6: (6, other_col),
             7: (0, outer_col), 8: (6, outer_col)}

    def settle(slot, q):
        row, col = spots[slot]
        when(routes[slot][1], lambda: place(packed, slot, parents, row, col, q))

    for slot in range(2, 9):

        @pl.when(jnp.logical_not(routes[slot][1]))
        def _(slot=slot):
            row, col = spots[slot]
            for pr in range(3):
                for pc in range(2):
                    parents[row + pr, col + pc] = jnp.zeros(parents.shape[2:], F32)

    def blank(ref, flag):
        @pl.when(jnp.logical_not(flag))
        def _():
            ref[...] = jnp.zeros(ref.shape, BF16)

    blank(own.at[low], has_down)
    blank(own.at[high], has_up)
    blank(oth.at[low], has_down)
    blank(oth.at[high], has_up)
    blank(outr.at[mid], has_outer)
    blank(outr.at[low], both_down)
    blank(outr.at[high], both_up)

    loads[3].wait()
    loads[4].wait()
    kind = lax.broadcasted_iota(jnp.int32, (32, 128), 1)
    for r in range(6):
        lists = fine_list[r]
        for c in range(4):
            mine = jnp.sum(jnp.where(kind == 4 * d + c, lists, 0), axis=1, keepdims=True)
            on_vec[r * 4 + c : r * 4 + c + 1, :] = jnp.sum(jnp.where(mine == kind, 1.0, 0.0), axis=0, keepdims=True)
    kind64 = lax.broadcasted_iota(jnp.int32, (32, 64), 1)
    for r in range(3):
        lists = par_list[r]
        for c in range(2):
            mine = jnp.sum(jnp.where(kind64 == 2 * d + c, lists, 0), axis=1, keepdims=True)
            row = 24 + r * 2 + c
            on_vec[row : row + 1, :] = jnp.sum(jnp.where(mine == kind, 1.0, 0.0), axis=0, keepdims=True)
    to_smem = pltpu.make_async_copy(on_vec, on, lsem.at[6])
    to_smem.start()

    def relay(q):
        block(2, q).wait_recv()
        for slot in (7, 8):
            start_block(slot, q)

    def relay_strips():
        strips[2].wait_recv()
        for slot in (7, 8):
            start(slot)

    def forward(q):
        for slot in (3, 4):
            arrive_block(slot, q)
            start_block(slot + 2, q)
            pl.when(hand_on[slot + 4])(lambda slot=slot: across(slot + 4, q).start())
        pl.when(direct)(lambda: relay(q))

    def near_side(columns_of):
        for which in range(2):
            pl.when(core == which)(
                lambda which=which: near_field(window, fine_ops, on, near, columns_of[which], 0, 6)
            )

    def relay_crossing(*qs):
        @pl.when(crossing)
        def _():
            for i in qs:
                relay(turn(i, 1 - y))

    def collect(half):
        for k in near_first:
            z_arrival(k, half).wait_recv()
            pass_on(k, half).start()

    for slot in (3, 4):
        arrive(slot)
        start(slot + 2)
    for c in range(2):
        widen(lambda r, c=c: own[r, c], window, range(10), 2 + 2 * c)
    to_smem.wait()
    loads[5].wait()
    near_field(window, fine_ops, on, near, OWN, 0, 2)
    to_far.wait()
    for k in near_first:
        z_send(k, 1).start()
    for half in range(2):
        pass_on(0, half).start()
    forward(turn(0))
    near_field(window, fine_ops, on, near, OWN, 2, 4)

    @pl.when(patient)
    def _():
        start(2)
        for i in range(pieces):
            start_block(2, turn(i))

    forward(turn(1))
    pl.when(direct)(relay_strips)
    near_field(window, fine_ops, on, near, OWN, 4, 6)
    collect(0)
    forward(turn(2))
    for slot in (1, 5, 6):
        arrive(slot)
    widen(lambda r: oth[r], window, range(10), 6 - 6 * core)
    near_side((RIGHT, LEFT))
    forward(turn(3))

    def gather_ops(chunk, carry):
        lanes = pl.ds(pl.multiple_of(chunk * 128, 128), 128)
        even, uneven = (opsg[i, lax.rem(chunk, ZN), chunk // ZN].astype(F32) for i in range(2))
        left = lax.broadcasted_iota(jnp.int32, even.shape, 1) < 64
        cos_ops[:, lanes] = jnp.where(left, even, pltpu.roll(uneven, 64, 1))
        sin_ops[:, lanes] = jnp.where(left, pltpu.roll(even, 64, 1), uneven)
        return carry

    variants = [(a, b) for a in range(2) for b in range(2)]

    def early(i, carry):
        q = turn(i)
        for slot in (1, 5, 6):
            arrive_block(slot, q)
        for slot in (1, 3, 4, 5, 6):
            settle(slot, q)
        lax.fori_loop(q * (PIECE // 128), (q + 1) * (PIECE // 128), gather_ops, 0)
        for a, b in variants:
            pl.when(jnp.logical_and(core == a, odd == b))(
                lambda a=a, b=b: far_early(parents, cos_ops, sin_ops, on, parent_in, a, b, q)
            )
        return carry

    for k in range(ZN):
        pass_on(k, 0).wait_recv()
    lax.fori_loop(0, half_pieces, early, 0)
    collect(1)

    def second_half():
        for k in range(ZN):
            pass_on(k, 1).wait_recv()
        lax.fori_loop(half_pieces, pieces, early, 0)

    pl.when(crossing)(relay_strips)
    relay_crossing(*range(pieces))
    pl.when(crossing)(second_half)
    for slot in (7, 8):
        arrive(slot)
    widen(lambda r: outr[r], window, range(10), 6 * core)
    near_side((LEFT, RIGHT))
    scale = interp.shape[0] / interp.shape[1]

    order = jnp.where(crossing, 1 - y, y)

    def last(i, carry):
        q = turn(i, order)
        settle(2, q)
        for slot in (7, 8):
            arrive_block(slot, q)
            settle(slot, q)
        for a, b in variants:
            pl.when(jnp.logical_and(core == a, odd == b))(
                lambda a=a, b=b: far_late(parents, cos_ops, sin_ops, on, parent_in, cosine, sine, child, a, b, q)
            )
        lanes = pl.ds(pl.multiple_of(q * PIECE, PIECE), PIECE)
        back = lax.dot_general(
            child[:, lanes], interp[:, lanes], (((1,), (1,)), ((), ())), preferred_element_type=F32
        )
        near[...] += (back * scale).reshape(near.shape)
        return carry

    lax.fori_loop(0, half_pieces, last, 0)
    pl.when(jnp.logical_not(crossing))(second_half)
    lax.fori_loop(half_pieces, pieces, last, 0)
    for r in range(6):
        for c in range(4):
            total = near[r * 4 + c]
            out[r, c, 0] = total[:4]
            out[r, c, 1] = total[4:]

    for copy in [z_send(k, half) for k in range(1, ZN) for half in range(2)] + [
        pass_on(k, half) for k in range(ZN) for half in range(2)
    ]:
        copy.wait_send()
    for slot in routes:
        when(routes[slot][0], lambda slot=slot: strips[slot].wait_send())

    def drain(q, carry):
        for slot in routes:
            sent_block(slot, q)
        for slot in (7, 8):
            pl.when(hand_on[slot])(lambda slot=slot: across(slot, q).wait_send())
        return carry

    lax.fori_loop(0, pieces, drain, 0)


def per_device(
    fine_out, interp, child_phase, fine_ops, parent_ops, fine_src, fine_op, parent_src, parent_op
):
    dp = interp.shape[1]
    kinds = fine_ops.shape[0]
    dma = pltpu.SemaphoreType.DMA
    hbm = pl.BlockSpec(memory_space=pl.ANY)
    vmem = pltpu.VMEM
    fine_list, par_list = (jnp.transpose(v, (0, 2, 1)) for v in (fine_op, parent_op))
    return pl.pallas_call(
        kernel,
        out_shape=jax.ShapeDtypeStruct(fine_out.shape, F32),
        in_specs=[hbm] * 7,
        out_specs=pl.BlockSpec(memory_space=pltpu.VMEM),
        scratch_shapes=[
            vmem((dp // PIECE, 9 * 48, PIECE), BF16),
            vmem((10, 2, 16, 512), BF16),
            vmem((10, 16, 512), BF16),
            vmem((10, 16, 512), BF16),
            vmem((2, ZN, 2, kinds, 128), BF16),
            vmem(fine_out.shape, BF16),
            vmem(parent_ops.shape, F32),
            vmem(interp.shape, BF16),
            vmem((4, dp), F32),
            vmem(fine_ops.shape, F32),
            vmem(fine_list.shape, jnp.int32),
            vmem(par_list.shape, jnp.int32),
            vmem((32, 128), F32),
            pltpu.SMEM((32, 128), F32),
            vmem((9, 6, 8, dp), F32),
            vmem((10, 8, 8, 512), F32),
            vmem((24, 8, 512), F32),
            vmem((6, 8, dp), F32),
            vmem((192, dp), BF16),
            vmem((4, dp), F32),
            vmem((4, dp), F32),
            vmem((kinds, dp), F32),
            vmem((kinds, dp), F32),
            dma((dp // PIECE, 8)), dma((dp // PIECE, 8)), dma((8,)), dma((8,)), dma((8,)), dma((dp // PIECE,)), dma((2,)),
            dma((2, ZN)), dma((2, ZN)), dma((2, ZN)), dma((2, ZN)),
        ],
        compiler_params=pltpu.CompilerParams(
            collective_id=0, has_side_effects=True, vmem_limit_bytes=56 * 1024 * 1024
        ),
        name="fmm",
    )(fine_out, parent_ops, interp, child_phase, fine_ops, fine_list, par_list)


def solution(mesh):
    in_specs = (
        P("patch", "dir", None, None, None),
        P(),
        P(),
        P(),
        P(None, None, "dir"),
        P("patch", None, None),
        P("patch", None, None),
        P("patch", None, None),
        P("patch", None, None),
    )
    out_specs = P("patch", "dir", None, None, None)
    return jax.shard_map(
        per_device, mesh=mesh, in_specs=in_specs, out_specs=out_specs, check_vma=False
    )
```
